256 devices in a mesh: centers: 256 (over y, z, x, core).
Axes of the slice: x: 4, y: 4, z: 8, core: 2. Of those that a mesh axis runs over, the one named last changes fastest.
Arguments:
- spectra: bfloat16 [131072, 2048], P('centers'), may hold values from -6 to 6
- targets: bfloat16 [131072, 300], P('centers'), may hold values from -6 to 6
- centers: bfloat16 [32768, 2048], P('centers'), may hold values from -6 to 6
- coefficients: float32 [32768, 300], P('centers'), may hold values from -3 to 3
- owners: int32 [2], replicated, may hold values from 0 to 255
- batch_rows: int32 [2, 256], replicated, may hold values from 0 to 511
Outputs:
- trained: float32 [32768, 300], P('centers')
- residuals: float32 [2, 256, 300], replicated
The draws below stay inside these ranges and needn't reach their ends.
Inputs may be any that keep to these rules, and one draw needn't show every extreme that they name: `owners`: a device index on the axis. `batch_rows`: rows may repeat.
All inputs are finite; a program needn't handle non-finite values.
Results may differ from the reference program's by a relative error of at most 0.0022.
Values may be sent and summed in bfloat16 or wider, within the bound.
No kernel may reach another device: no remote copies, remote signals or barrier semaphores. Data moves between devices by JAX's collectives and lax.ppermute only.
A program may use at most 64 MiB of HBM per device.

```python
import math
import jax
import jax.numpy as jnp
from jax import lax

F = 2048
OUT = 300
CDEV = 128
SDEV = 512
B = 256
ITERS = 2
NC = 32768
NS = 131072
N_CENTERS = 256


def place_ends(result, own_key, least, top_value):
    longest = result.shape.index(max(result.shape))
    spots = []
    for shift in (0, 1):
        where = [jax.random.randint(jax.random.fold_in(own_key, axis), (), 0, length) for axis, length in enumerate(result.shape)]
        where[longest] = (where[longest] + shift) % result.shape[longest]
        spots.append(tuple(where))
    return result.at[spots[0]].set(least).at[spots[1]].set(top_value)


def level_of(key, dims, shards, smallest, largest):
    def one(dim, blocks):
        heights = jax.random.uniform(jax.random.fold_in(jax.random.fold_in(key, 6), dim), (blocks,), jnp.float32, smallest / len(shards), largest / len(shards))
        return jnp.repeat(jnp.exp(heights), dims[dim] // blocks).reshape((-1,) + (1,) * (len(dims) - dim - 1))

    level = one(*shards[0])
    for cut in shards[1:]:
        level = level * one(*cut)
    return level


def scatter_about(own_key, dims, deviation, limit, cuts=(), dtype=jnp.bfloat16):
    drawn = deviation * jax.random.normal(own_key, dims, jnp.float32)
    if cuts:
        drawn = drawn * level_of(own_key, dims, cuts, -0.22, 0.18)
    return jnp.clip(drawn, -limit, limit).astype(dtype)


def setup_inputs(seed: int = 0) -> dict:
    keys = jax.random.split(jax.random.key(seed), 7)
    spectra = scatter_about(keys[0], (NS, F), 1.0, 6.0, ((0, 256),))
    targets = scatter_about(keys[1], (NS, OUT), 1.0, 6.0, ((0, 256),))
    centers = scatter_about(keys[2], (NC, F), 1.0, 6.0, ((0, 256),))
    coefficients = scatter_about(keys[3], (NC, OUT), 0.5, 3.0, ((0, 256),), jnp.float32)
    owners = jax.random.randint(keys[4], (ITERS,), 0, N_CENTERS).astype(jnp.int32)
    batch_rows = place_ends(jax.random.randint(keys[5], (ITERS, B), 0, SDEV), jax.random.fold_in(keys[5], 1), 0, SDEV - 1).astype(jnp.int32)
    return {"spectra": spectra, "targets": targets, "centers": centers, "coefficients": coefficients, "owners": owners, "batch_rows": batch_rows}


EPSILON = 1e-06
STEP_RATE = 0.2

def kernel_tile(batch_spectra, block):
    dots = lax.dot_general(batch_spectra, block, (((1,), (1,)), ((), ())), preferred_element_type=jnp.float32)
    batch_norms = jnp.sqrt(lax.optimization_barrier(jnp.sum(jnp.square(batch_spectra.astype(jnp.float32)), axis=1)) + EPSILON)
    center_norms = jnp.sqrt(lax.optimization_barrier(jnp.sum(jnp.square(block.astype(jnp.float32)), axis=1)) + EPSILON)
    scaled = dots / (batch_norms[:, None] * center_norms[None, :]) * math.sqrt(F)
    return (scaled + scaled * scaled * scaled / 3.0).astype(jnp.bfloat16)

def reference(spectra, targets, centers, coefficients, owners, batch_rows):
    blocks = centers.reshape(N_CENTERS, CDEV, F)
    weights = coefficients.reshape(N_CENTERS, CDEV, OUT)
    root_scale = math.sqrt(CDEV * N_CENTERS)
    history = []
    for iteration in range(ITERS):
        chosen = (owners[iteration] * SDEV + batch_rows[iteration]).astype(jnp.int32)
        batch_spectra = jnp.take(spectra, chosen, axis=0)
        batch_target = jnp.take(targets, chosen, axis=0).astype(jnp.float32)
        tiles = lax.map(lambda block: kernel_tile(batch_spectra, block), blocks)
        wide_tiles = tiles.astype(jnp.float32)
        prediction = jnp.einsum('kbc,kco->bo', wide_tiles, weights, precision=lax.Precision.HIGHEST) / root_scale
        residual = prediction - batch_target
        update = jnp.einsum('kbc,bo->kco', wide_tiles, residual, precision=lax.Precision.HIGHEST)
        weights = weights - STEP_RATE / root_scale * update
        history.append(residual)
    return (weights.reshape(N_CENTERS * CDEV, OUT), jnp.stack(history))
```

```python
import math

import jax
import jax.numpy as jnp
from jax import lax
from jax.sharding import Mesh
from jax.sharding import PartitionSpec as P

ITERS = 2
AXES = ("y", "z", "x", "core")
PLANE = ("y", "x")
EPSILON = 1e-06
STEP_RATE = 0.2
PAIR = [(0, 1), (1, 0)]


def swap(value):
    return lax.ppermute(value, "core", PAIR)


def exchange(blocks, axes):
    return lax.all_to_all(blocks, axes, 0, 0, tiled=True)


def copies(value, axes):
    size = lax.axis_size(axes)
    return exchange(jnp.broadcast_to(value[None], (size, *value.shape)), axes)


def rows_of(array, rows):
    return array.at[rows].get(mode="promise_in_bounds")


def norms_of(value):
    return jnp.sqrt(jnp.sum(jnp.square(value.astype(jnp.float32)), axis=1) + EPSILON)


def body(spectra, targets, centers, coefficients, owners, batch_rows):
    features = centers.shape[1]
    outs = coefficients.shape[1]
    batch = batch_rows.shape[1]
    half = batch // 2
    factor = math.sqrt(features)
    total = centers.shape[0] * lax.axis_size(AXES)
    root_scale = math.sqrt(total)
    sizes = [lax.axis_size(name) for name in AXES]
    y, z, x, core = (lax.axis_index(name) for name in AXES)
    root_core = owners % sizes[3]
    root_x = owners // sizes[3] % sizes[2]
    root_z = owners // (sizes[3] * sizes[2]) % sizes[1]
    root_y = owners // (sizes[3] * sizes[2] * sizes[1])
    root_plane = root_y * sizes[2] + root_x
    own_root = root_core == core
    on_root = (root_y == y) & (root_z == z) & (root_x == x)

    both_centers = jnp.concatenate([centers, swap(centers)])
    both_coefficients = jnp.concatenate([coefficients, swap(coefficients)])
    center_norms = norms_of(both_centers)

    halves = batch_rows.reshape(ITERS, 2, half)
    kept_rows = jnp.where(core == 0, halves[:, 0], halves[:, 1])
    sent_rows = jnp.where(core == 0, halves[:, 1], halves[:, 0])
    kept = rows_of(spectra, kept_rows)
    came = swap(rows_of(spectra, sent_rows))
    mine = jnp.where(own_root[:, None, None], kept, came)
    kept_targets = rows_of(targets, kept_rows)
    came_targets = swap(rows_of(targets, sent_rows))
    mine_targets = jnp.where(own_root[:, None, None], kept_targets, came_targets)

    plane = sizes[0] * sizes[2]
    each = half // plane
    blocks = mine.reshape(ITERS, plane, each, features)
    scattered = exchange(jnp.swapaxes(blocks, 0, 1), PLANE)
    piece = jnp.stack(
        [lax.dynamic_index_in_dim(scattered, root_plane[t], 0, False)[t] for t in range(ITERS)]
    )
    along = copies(piece, "z")
    piece = jnp.stack(
        [lax.dynamic_index_in_dim(along, root_z[t], 0, False)[t] for t in range(ITERS)]
    )
    gathered = copies(piece, PLANE)
    spectra_half = jnp.swapaxes(gathered, 0, 1).reshape(ITERS * half, features)

    dots = lax.dot_general(
        spectra_half, both_centers, (((1,), (1,)), ((), ())), preferred_element_type=jnp.float32
    )
    scaled = dots / (norms_of(spectra_half)[:, None] * center_norms[None, :]) * factor
    tile = (scaled + scaled * scaled * scaled / 3.0).astype(jnp.bfloat16)
    other = swap(jnp.roll(tile, centers.shape[0], axis=1))
    tile_0, tile_1 = tile[:half], tile[half:]

    partial = (
        jnp.dot(
            tile.astype(jnp.float32),
            both_coefficients,
            precision=lax.Precision.HIGHEST,
            preferred_element_type=jnp.float32,
        )
        / root_scale
    ).reshape(ITERS, half, outs)
    held = jnp.where(on_root[:, None, None], mine_targets, 0).astype(jnp.float32)
    partial = partial - held
    gram = lax.dot_general(
        tile_1,
        jnp.concatenate([tile_0, other[:half]]),
        (((1,), (1,)), ((), ())),
        preferred_element_type=jnp.float32,
    )
    lines = jnp.concatenate([partial[0], partial[1], gram], axis=1)
    own = exchange(lines.reshape(plane, each, -1), PLANE).sum(axis=0)
    own = copies(own, "z").sum(axis=0)
    whole = copies(own, PLANE).reshape(half, -1)
    whole_other = swap(whole)

    first, second = whole[:, :outs], whole_other[:, :outs]
    mixed = jnp.concatenate([whole[:, 2 * outs :], jnp.roll(whole_other[:, 2 * outs :], half, axis=1)])
    later = jnp.concatenate([whole[:, outs : 2 * outs], whole_other[:, outs : 2 * outs]])
    residual_0 = jnp.concatenate([first, second])
    residual_1 = later - STEP_RATE / total * jnp.dot(
        mixed, residual_0, precision=lax.Precision.HIGHEST, preferred_element_type=jnp.float32
    )
    own_centers = centers.shape[0]
    tiles = jnp.concatenate(
        [tile_0[:, :own_centers], other[:half, :own_centers], tile_1[:, :own_centers], other[half:, :own_centers]]
    )
    update = lax.dot_general(
        tiles.astype(jnp.float32),
        jnp.concatenate([residual_0, residual_1]),
        (((0,), (0,)), ((), ())),
        precision=lax.Precision.HIGHEST,
        preferred_element_type=jnp.float32,
    )
    trained = coefficients - STEP_RATE / root_scale * update
    residuals = jnp.stack([residual_0, residual_1]).reshape(ITERS, 2, half, outs)
    residuals = jnp.where(core == 0, residuals, residuals[:, ::-1]).reshape(ITERS, batch, outs)
    return trained, residuals


def solution(mesh):
    torus = Mesh(mesh.devices.reshape(4, 8, 4, 2), AXES)
    return jax.shard_map(
        body,
        mesh=torus,
        in_specs=(P(AXES, None), P(AXES, None), P(AXES, None), P(AXES, None), P(), P()),
        out_specs=(P(AXES, None), P()),
        check_vma=False,
    )
```

```python
import functools
import math

import jax
import jax.numpy as jnp
from jax import lax
from jax.experimental import pallas as pl
from jax.experimental.pallas import tpu as pltpu
from jax.sharding import Mesh
from jax.sharding import PartitionSpec as P

ITERS = 2
AXES = ("y", "z", "x", "core")
PLANE = ("y", "x")
EPSILON = 1e-06
STEP_RATE = 0.2
PAIR = [(0, 1), (1, 0)]
Z_MASKS = (1, 2, 6)
HIGHEST = lax.Precision.HIGHEST
NT = (((1,), (1,)), ((), ()))


def swap(value):
    return lax.ppermute(value, "core", PAIR)


def exchange(blocks, axes):
    return lax.all_to_all(blocks, axes, 0, 0, tiled=True)


def copies(value, axes):
    size = lax.axis_size(axes)
    return exchange(jnp.broadcast_to(value[None], (size, *value.shape)), axes)


def squares(value):
    return jnp.sum(jnp.square(value.astype(jnp.float32)), axis=1)


def aligned(size):
    return -(-size // 8) * 8


def tile_kernel(batch, own, other, own_norms, other_norms, tile, *, each, factor):
    lines = batch[...]
    norms = jnp.sqrt(
        jnp.sum(jnp.square(lines.astype(jnp.float32)), axis=1, keepdims=True) + EPSILON
    )
    count = lines.shape[0] // ITERS
    width = own.shape[0]
    for at, (centers, center_norms) in enumerate(((own, own_norms), (other, other_norms))):
        dots = lax.dot_general(lines, centers[...], NT, preferred_element_type=jnp.float32)
        scaled = dots / (norms * center_norms[...]) * factor
        value = scaled + scaled * scaled * scaled / 3.0
        value = value.reshape(count // each, ITERS, each, width)
        for t in range(ITERS):
            tile[t, :, at * width : (at + 1) * width] = (
                value[:, t].reshape(count, width).astype(tile.dtype)
            )


def partial_kernel(core, tile, came, own, other, held, lines, *, root_scale):
    outs, width = own.shape
    count = tile.shape[1]
    step = aligned(outs)
    lines[...] = jnp.zeros_like(lines)
    for t in range(ITERS):
        total = lax.dot_general(
            own[...],
            tile[t, :, :width].astype(jnp.float32),
            NT,
            precision=HIGHEST,
            preferred_element_type=jnp.float32,
        ) + lax.dot_general(
            other[...],
            tile[t, :, width:].astype(jnp.float32),
            NT,
            precision=HIGHEST,
            preferred_element_type=jnp.float32,
        )
        lines[t * step : t * step + outs, :] = total / root_scale - held[
            :, t * count : (t + 1) * count
        ].astype(jnp.float32)
    mine = tile[0]
    theirs = jnp.concatenate([came[0, :, width:], came[0, :, :width]], axis=1)
    later = tile[1]
    gram = [
        lax.dot_general(value, later, NT, preferred_element_type=jnp.float32)
        for value in (mine, theirs)
    ]
    is_first = core[0] == 0
    lines[2 * step : 2 * step + count, :] = jnp.where(is_first, gram[0], gram[1])
    lines[2 * step + count : 2 * step + 2 * count, :] = jnp.where(is_first, gram[1], gram[0])


def finish_kernel(core, mine, other, tile, came, coefficients, trained, residuals, *, total):
    outs, width = coefficients.shape
    count = mine.shape[1]
    step = aligned(outs)
    is_first = core[0] == 0

    def both(start, size):
        kept, sent = mine[start : start + size, :], other[start : start + size, :]
        return jnp.concatenate(
            [jnp.where(is_first, kept, sent), jnp.where(is_first, sent, kept)], axis=1
        )

    first = both(0, outs)
    gram = both(2 * step, 2 * count)
    second = both(step, outs) - STEP_RATE / total * jnp.dot(
        first, gram, precision=HIGHEST, preferred_element_type=jnp.float32
    )
    update = None
    for t, residual in enumerate((first, second)):
        residuals[:, t, :] = residual
        kept = tile[t, :, :width].astype(jnp.float32)
        sent = came[t, :, width:].astype(jnp.float32)
        rows = jnp.concatenate(
            [jnp.where(is_first, kept, sent), jnp.where(is_first, sent, kept)], axis=0
        )
        term = jnp.dot(residual, rows, precision=HIGHEST, preferred_element_type=jnp.float32)
        update = term if update is None else update + term
    trained[...] = coefficients[...] - STEP_RATE / math.sqrt(total) * update


def whole_specs(kinds):
    return [pl.BlockSpec(memory_space=kind) for kind in kinds]


def call(kernel, out_shape, operands, scalars=0):
    kinds = [pltpu.SMEM] * scalars + [pltpu.VMEM] * (len(operands) - scalars)
    outs = out_shape if isinstance(out_shape, tuple) else (out_shape,)
    specs = tuple(whole_specs([pltpu.VMEM] * len(outs)))
    operands = operands[:scalars] + tuple(
        pltpu.with_memory_space_constraint(value, pltpu.VMEM) for value in operands[scalars:]
    )
    return pl.pallas_call(
        kernel,
        in_specs=whole_specs(kinds),
        out_specs=specs if isinstance(out_shape, tuple) else specs[0],
        out_shape=out_shape,
    )(*operands)


def body(spectra, targets, centers, coefficients, owners, batch_rows):
    width, features = centers.shape
    held_rows = targets.shape[0]
    outs = coefficients.shape[1]
    batch = batch_rows.shape[1]
    half = batch // 2
    factor = math.sqrt(features)
    total = width * lax.axis_size(AXES)
    root_scale = math.sqrt(total)
    sizes = [lax.axis_size(name) for name in AXES]
    y, z, x, core = (lax.axis_index(name) for name in AXES)
    roots = [owners[t] for t in range(ITERS)]
    bits = [size.bit_length() - 1 for size in sizes]
    root_core = [root & (sizes[3] - 1) for root in roots]
    root_x = [root >> bits[3] & (sizes[2] - 1) for root in roots]
    root_z = [root >> (bits[3] + bits[2]) & (sizes[1] - 1) for root in roots]
    root_y = [root >> (bits[3] + bits[2] + bits[1]) for root in roots]
    root_plane = [root_y[t] * sizes[2] + root_x[t] for t in range(ITERS)]
    own_root = [root_core[t] == core for t in range(ITERS)]
    on_root = [(root_y[t] == y) & (root_z[t] == z) & (root_x[t] == x) for t in range(ITERS)]
    plane = sizes[0] * sizes[2]
    each = half // plane

    halves = batch_rows.reshape(ITERS, 2, half)
    kept_rows = jnp.where(core == 0, halves[:, 0], halves[:, 1])
    sent_rows = jnp.where(core == 0, halves[:, 1], halves[:, 0])

    def spread(kept, sent, own):
        slots = kept.shape[0]

        def take(rows):
            order = jnp.swapaxes(rows.reshape(slots, plane, each), 0, 1).reshape(-1)
            return spectra.at[order].get(mode="promise_in_bounds")

        mine = take(kept).reshape(plane, slots, each, features)
        came = swap(take(sent)).reshape(plane, slots, each, features)
        return exchange(jnp.where(own.reshape(1, slots, 1, 1), mine, came), PLANE)

    def pick(scattered, slot):
        return jnp.stack(
            [
                lax.dynamic_index_in_dim(
                    scattered[:, slot[t]], root_plane[t], 0, False, allow_negative_indices=False
                )
                for t in range(ITERS)
            ]
        )

    def spread_one():
        later = on_root[1]
        return pick(
            spread(
                jnp.where(later, kept_rows[1], kept_rows[0])[None],
                jnp.where(later, sent_rows[1], sent_rows[0])[None],
                jnp.where(later, own_root[1], own_root[0])[None],
            ),
            (0, 0),
        )

    def spread_both():
        return pick(spread(kept_rows, sent_rows, jnp.stack(own_root)), (0, 1))

    piece = lax.cond(roots[0] >> bits[3] != roots[1] >> bits[3], spread_one, spread_both)

    apart = [z ^ root_z[t] for t in range(ITERS)]
    high = [apart[t] >> 2 for t in range(ITERS)]
    rest = [apart[t] ^ (Z_MASKS[2] * high[t]) for t in range(ITERS)]
    reached = [
        [rest[t] + high[t] == 0 for t in range(ITERS)],
        [(rest[t] >> 1) + high[t] == 0 for t in range(ITERS)],
        [high[t] == 0 for t in range(ITERS)],
    ]
    for mask, have in zip(Z_MASKS, reached):
        arrived = lax.ppermute(piece, "z", [(i, i ^ mask) for i in range(sizes[1])])
        piece = jnp.where(jnp.stack(have).reshape(ITERS, 1, 1), piece, arrived)
    gathered = copies(piece, PLANE).reshape(ITERS * half, features)

    def targets_of(rows):
        spots = (
            lax.broadcasted_iota(jnp.int32, (held_rows, ITERS * half), 0) == rows.reshape(1, -1)
        ).astype(targets.dtype)
        return lax.dot_general(
            targets, spots, (((0,), (0,)), ((), ())), preferred_element_type=jnp.float32
        ).astype(targets.dtype)

    def by_iteration(flags):
        return jnp.repeat(jnp.stack(flags), half).reshape(1, -1)

    held = jnp.where(by_iteration(own_root), targets_of(kept_rows), swap(targets_of(sent_rows)))
    held = jnp.where(by_iteration(on_root), held, 0).astype(targets.dtype)

    turned = coefficients.T
    turned_other = swap(turned)
    other_centers = swap(centers)
    norms = [jnp.sqrt(squares(value) + EPSILON).reshape(1, -1) for value in (centers, other_centers)]

    tile = call(
        functools.partial(tile_kernel, each=each, factor=factor),
        pltpu.VMEM((ITERS, half, 2 * width), jnp.bfloat16),
        (gathered, centers, other_centers, *norms),
    )
    came = swap(tile)
    at = core.reshape(1)
    height = -(-(2 * aligned(outs) + batch) // (8 * plane)) * 8
    lines = call(
        functools.partial(partial_kernel, root_scale=root_scale),
        pltpu.VMEM((plane * height, half), jnp.float32),
        (at, tile, came, turned, turned_other, held),
        scalars=1,
    )
    own = exchange(lines.reshape(plane, height, half), PLANE).sum(axis=0)
    own = copies(own, "z").sum(axis=0)
    whole = copies(own, PLANE).reshape(plane * height, half)
    trained, residuals = call(
        functools.partial(finish_kernel, total=total),
        (
            jax.ShapeDtypeStruct((outs, width), jnp.float32),
            jax.ShapeDtypeStruct((outs, ITERS, batch), jnp.float32),
        ),
        (at, whole, swap(whole), tile, came, turned),
        scalars=1,
    )
    return trained.T, jnp.transpose(residuals, (1, 2, 0))


def solution(mesh):
    torus = Mesh(mesh.devices.reshape(4, 8, 4, 2), AXES)
    return jax.shard_map(
        body,
        mesh=torus,
        in_specs=(P(AXES, None), P(AXES, None), P(AXES, None), P(AXES, None), P(), P()),
        out_specs=(P(AXES, None), P()),
        check_vma=False,
    )
```

```python
import functools
import math

import jax
import jax.numpy as jnp
from jax import lax
from jax.experimental import pallas as pl
from jax.experimental.pallas import tpu as pltpu
from jax.sharding import Mesh
from jax.sharding import PartitionSpec as P

ITERS = 2
AXES = ("y", "z", "x", "core")
PLANE = ("y", "x")
EPSILON = 1e-06
STEP_RATE = 0.2
PAIR = [(0, 1), (1, 0)]
Z_MASKS = (1, 2, 7)
SCRATCH = 16 << 20
HIGHEST = lax.Precision.HIGHEST
NT = (((1,), (1,)), ((), ()))


def swap(value):
    return lax.ppermute(value, "core", PAIR)


def exchange(blocks, axes):
    return lax.all_to_all(blocks, axes, 0, 0, tiled=True)


def place(device, sizes):
    bits = [size.bit_length() - 1 for size in sizes]
    core = device & (sizes[3] - 1)
    x = device >> bits[3] & (sizes[2] - 1)
    z = device >> (bits[3] + bits[2]) & (sizes[1] - 1)
    return device >> (bits[3] + bits[2] + bits[1]), z, x, core


def chosen(rows, held, own):
    spots = lax.broadcasted_iota(jnp.int32, (held, rows.shape[1]), 0) == rows
    return jnp.where(spots & own, 1.0, 0.0).astype(jnp.bfloat16)


def halves_of(batch_rows, t, core):
    rows = batch_rows[pl.ds(t, 1), :] if not isinstance(t, int) else batch_rows[t : t + 1, :]
    half = rows.shape[1] // 2
    first, second = rows[:, :half], rows[:, half:]
    return jnp.where(core == 0, first, second), jnp.where(core == 0, second, first)


def copies(value, axes):
    size = lax.axis_size(axes)
    return exchange(jnp.broadcast_to(value[None], (size, *value.shape)), axes)


def squares(value):
    return jnp.sum(jnp.square(value.astype(jnp.float32)), axis=1)


def aligned(size):
    return -(-size // 8) * 8


def rows_kernel(device, owners, batch_rows, spectra, kept, sent, *flag, sizes):
    here = device[0]
    core = here & (sizes[3] - 1)
    plane, slots, each, features = kept.shape
    if flag:
        flag[0][0] = jnp.where(owners[0] // 2 != owners[1] // 2, 1, 0)
    for slot in range(slots):
        t = slot if slots > 1 else jnp.where(owners[1] // 2 == here // 2, 1, 0)
        own = owners[t] == here
        for rows, out in zip(halves_of(batch_rows, t, core), (kept, sent)):
            value = lax.dot_general(
                chosen(rows, spectra.shape[0], own),
                spectra[...],
                (((0,), (0,)), ((), ())),
                preferred_element_type=jnp.float32,
            )
            out[:, slot] = value.astype(out.dtype).reshape(plane, each, features)


def targets_kernel(device, owners, batch_rows, targets, kept, sent, *, sizes):
    here = device[0]
    core = here & (sizes[3] - 1)
    half = batch_rows.shape[1] // 2
    for t in range(ITERS):
        own = owners[t] == here
        for rows, out in zip(halves_of(batch_rows, t, core), (kept, sent)):
            out[:, t * half : (t + 1) * half] = jnp.dot(
                targets[...],
                chosen(rows, targets.shape[1], own),
                preferred_element_type=jnp.float32,
            ).astype(out.dtype)


def pick_kernel(device, owners, scattered, piece, *, sizes):
    _, z, _, _ = place(device[0], sizes)
    slots = scattered.shape[1]
    for t in range(ITERS):
        root_y, root_z, root_x, _ = place(owners[t], sizes)
        block = scattered[root_y * sizes[2] + root_x, t if slots > 1 else 0]
        piece[t] = jnp.where(root_z == z, block, jnp.zeros_like(block))


def spread_kernel(piece, arrived, out):
    out[...] = jnp.broadcast_to((piece[...] + arrived[...])[None], out.shape)


def tile_kernel(batch, own, other, own_norms, other_norms, tile, *, each, factor):
    lines = batch[...]
    norms = jnp.sqrt(
        jnp.sum(jnp.square(lines.astype(jnp.float32)), axis=1, keepdims=True) + EPSILON
    )
    count = lines.shape[0] // ITERS
    width = own.shape[0]
    for at, (centers, center_norms) in enumerate(((own, own_norms), (other, other_norms))):
        dots = lax.dot_general(lines, centers[...], NT, preferred_element_type=jnp.float32)
        scaled = dots / (norms * center_norms[...]) * factor
        value = scaled + scaled * scaled * scaled / 3.0
        value = value.reshape(count // each, ITERS, each, width)
        for t in range(ITERS):
            tile[t, :, at * width : (at + 1) * width] = (
                value[:, t].reshape(count, width).astype(tile.dtype)
            )


def partial_kernel(core, tile, came, own, other, kept, arrived, lines, *, root_scale):
    outs, width = own.shape
    count = tile.shape[1]
    step = aligned(outs)
    lines[...] = jnp.zeros_like(lines)
    held = kept[...].astype(jnp.float32) + arrived[...].astype(jnp.float32)
    for t in range(ITERS):
        total = lax.dot_general(
            own[...],
            tile[t, :, :width].astype(jnp.float32),
            NT,
            precision=HIGHEST,
            preferred_element_type=jnp.float32,
        ) + lax.dot_general(
            other[...],
            tile[t, :, width:].astype(jnp.float32),
            NT,
            precision=HIGHEST,
            preferred_element_type=jnp.float32,
        )
        lines[t * step : t * step + outs, :] = (
            total / root_scale - held[:, t * count : (t + 1) * count]
        )
    mine = tile[0]
    theirs = jnp.concatenate([came[0, :, width:], came[0, :, :width]], axis=1)
    later = tile[1]
    gram = [
        lax.dot_general(value, later, NT, preferred_element_type=jnp.float32)
        for value in (mine, theirs)
    ]
    is_first = core[0] == 0
    lines[2 * step : 2 * step + count, :] = jnp.where(is_first, gram[0], gram[1])
    lines[2 * step + count : 2 * step + 2 * count, :] = jnp.where(is_first, gram[1], gram[0])


def finish_kernel(core, mine, other, tile, came, coefficients, trained, residuals, *, total):
    outs, width = coefficients.shape
    count = mine.shape[1]
    step = aligned(outs)
    is_first = core[0] == 0

    def both(start, size):
        kept, sent = mine[start : start + size, :], other[start : start + size, :]
        return jnp.concatenate(
            [jnp.where(is_first, kept, sent), jnp.where(is_first, sent, kept)], axis=1
        )

    first = both(0, outs)
    gram = both(2 * step, 2 * count)
    second = both(step, outs) - STEP_RATE / total * jnp.dot(
        first, gram, precision=HIGHEST, preferred_element_type=jnp.float32
    )
    update = None
    for t, residual in enumerate((first, second)):
        residuals[:, t, :] = residual
        kept = tile[t, :, :width].astype(jnp.float32)
        sent = came[t, :, width:].astype(jnp.float32)
        rows = jnp.concatenate(
            [jnp.where(is_first, kept, sent), jnp.where(is_first, sent, kept)], axis=0
        )
        term = jnp.dot(residual, rows, precision=HIGHEST, preferred_element_type=jnp.float32)
        update = term if update is None else update + term
    trained[...] = coefficients[...] - STEP_RATE / math.sqrt(total) * update


def call(kernel, out_shape, operands, scalars=0, out_kinds=None):
    outs = out_shape if isinstance(out_shape, tuple) else (out_shape,)
    out_kinds = out_kinds or [pltpu.VMEM] * len(outs)
    specs = tuple(pl.BlockSpec(memory_space=kind) for kind in out_kinds)
    kinds = [pltpu.SMEM] * scalars + [pltpu.VMEM] * (len(operands) - scalars)
    operands = operands[:scalars] + tuple(
        pltpu.with_memory_space_constraint(value, pltpu.VMEM) for value in operands[scalars:]
    )
    return pl.pallas_call(
        kernel,
        in_specs=[pl.BlockSpec(memory_space=kind) for kind in kinds],
        out_specs=specs if isinstance(out_shape, tuple) else specs[0],
        out_shape=out_shape,
        compiler_params=pltpu.CompilerParams(vmem_limit_bytes=SCRATCH),
    )(*operands)


def body(spectra, targets, centers, coefficients, owners, batch_rows):
    width, features = centers.shape
    outs = coefficients.shape[1]
    batch = batch_rows.shape[1]
    half = batch // 2
    total = width * lax.axis_size(AXES)
    sizes = tuple(lax.axis_size(name) for name in AXES)
    plane = sizes[0] * sizes[2]
    each = half // plane
    device = lax.axis_index(AXES).reshape(1)
    core = lax.axis_index("core").reshape(1)
    narrow = jnp.bfloat16

    def rows_for(slots):
        block = pltpu.VMEM((plane, slots, each, features), narrow)
        flag = (jax.ShapeDtypeStruct((1,), jnp.int32),) if slots == 1 else ()
        return call(
            functools.partial(rows_kernel, sizes=sizes),
            (block, block) + flag,
            (device, owners, batch_rows, spectra),
            scalars=2,
            out_kinds=[pltpu.VMEM, pltpu.VMEM] + [pltpu.SMEM] * len(flag),
        )

    def spread(kept, sent):
        scattered = exchange(kept + swap(sent), PLANE)
        return call(
            functools.partial(pick_kernel, sizes=sizes),
            pltpu.VMEM((ITERS, each, features), narrow),
            (device, owners, scattered),
            scalars=2,
        )

    kept, sent, apart = rows_for(1)
    piece = lax.cond(apart[0] != 0, lambda: spread(kept, sent), lambda: spread(*rows_for(2)))

    arrived = None
    for mask in Z_MASKS:
        piece = piece if arrived is None else piece + arrived
        arrived = lax.ppermute(piece, "z", [(i, i ^ mask) for i in range(sizes[1])])
    spread_out = call(
        spread_kernel,
        pltpu.VMEM((plane, ITERS, each, features), narrow),
        (piece, arrived),
    )
    gathered = exchange(spread_out, PLANE).reshape(ITERS * half, features)

    shown = pltpu.VMEM((outs, ITERS * half), narrow)
    kept_targets, sent_targets = call(
        functools.partial(targets_kernel, sizes=sizes),
        (shown, shown),
        (device, owners, batch_rows, targets.T),
        scalars=2,
    )
    came_targets = swap(sent_targets)

    turned = coefficients.T
    turned_other = swap(turned)
    other_centers = swap(centers)
    norms = [jnp.sqrt(squares(value) + EPSILON).reshape(1, -1) for value in (centers, other_centers)]

    tile = call(
        functools.partial(tile_kernel, each=each, factor=math.sqrt(features)),
        pltpu.VMEM((ITERS, half, 2 * width), narrow),
        (gathered, centers, other_centers, *norms),
    )
    came = swap(tile)
    height = -(-(2 * aligned(outs) + batch) // (8 * plane)) * 8
    lines = call(
        functools.partial(partial_kernel, root_scale=math.sqrt(total)),
        pltpu.VMEM((plane * height, half), jnp.float32),
        (core, tile, came, turned, turned_other, kept_targets, came_targets),
        scalars=1,
    )
    own = exchange(lines.reshape(plane, height, half), PLANE).sum(axis=0)
    own = copies(own, "z").sum(axis=0)
    whole = copies(own, PLANE).reshape(plane * height, half)
    trained, residuals = call(
        functools.partial(finish_kernel, total=total),
        (
            jax.ShapeDtypeStruct((outs, width), jnp.float32),
            jax.ShapeDtypeStruct((outs, ITERS, batch), jnp.float32),
        ),
        (core, whole, swap(whole), tile, came, turned),
        scalars=1,
    )
    return trained.T, jnp.transpose(residuals, (1, 2, 0))


def solution(mesh):
    torus = Mesh(mesh.devices.reshape(4, 8, 4, 2), AXES)
    return jax.shard_map(
        body,
        mesh=torus,
        in_specs=(P(AXES, None), P(AXES, None), P(AXES, None), P(AXES, None), P(), P()),
        out_specs=(P(AXES, None), P()),
        check_vma=False,
    )
```

```python
import functools
import math

import jax
import jax.numpy as jnp
from jax import lax
from jax.experimental import pallas as pl
from jax.experimental.pallas import tpu as pltpu
from jax.sharding import Mesh
from jax.sharding import PartitionSpec as P

ITERS = 2
AXES = ("y", "z", "x", "core")
PLANE = ("y", "x")
EPSILON = 1e-06
STEP_RATE = 0.2
PAIR = [(0, 1), (1, 0)]
Z_MASKS = (1, 2, 7)
SCRATCH = 16 << 20
CHUNKS = 4
HIGHEST = lax.Precision.HIGHEST
NT = (((1,), (1,)), ((), ()))


def swap(value):
    return lax.ppermute(value, "core", PAIR)


def exchange(blocks, axes):
    return lax.all_to_all(blocks, axes, 0, 0, tiled=True)


def place(device, sizes):
    bits = [size.bit_length() - 1 for size in sizes]
    core = device & (sizes[3] - 1)
    x = device >> bits[3] & (sizes[2] - 1)
    z = device >> (bits[3] + bits[2]) & (sizes[1] - 1)
    return device >> (bits[3] + bits[2] + bits[1]), z, x, core


def chosen(rows, held, own):
    spots = lax.broadcasted_iota(jnp.int32, (held, rows.shape[1]), 0) == rows
    return jnp.where(spots & own, 1.0, 0.0).astype(jnp.bfloat16)


def halves_of(batch_rows, t, core):
    rows = batch_rows[pl.ds(t, 1), :] if not isinstance(t, int) else batch_rows[t : t + 1, :]
    half = rows.shape[1] // 2
    first, second = rows[:, :half], rows[:, half:]
    return jnp.where(core == 0, first, second), jnp.where(core == 0, second, first)


def copies(value, axes):
    size = lax.axis_size(axes)
    return exchange(jnp.broadcast_to(value[None], (size, *value.shape)), axes)


def squares(value):
    return jnp.sum(jnp.square(value.astype(jnp.float32)), axis=1)


def aligned(size):
    return -(-size // 8) * 8


def rows_kernel(device, owners, batch_rows, spectra, kept, sent, *rest, sizes):
    flag, (lines, listed, arrivals) = rest[:-3], rest[-3:]
    here = device[0]
    core = here & (sizes[3] - 1)
    plane, slots, each, features = kept.shape
    chunk = features // CHUNKS
    listing = pltpu.make_async_copy(batch_rows, listed, arrivals.at[CHUNKS])
    listing.start()
    loads = []
    for at in range(CHUNKS):
        columns = slice(at * chunk, (at + 1) * chunk)
        load = pltpu.make_async_copy(spectra.at[:, columns], lines.at[:, columns], arrivals.at[at])
        load.start()
        loads.append(load)
    if flag:
        same_chip = owners[0] >> 1 == owners[1] >> 1
        same_z = place(owners[0], sizes)[1] == place(owners[1], sizes)[1]
        flag[0][0] = jnp.where(same_chip, 0, jnp.where(same_z, 1, 2))
    listing.wait()
    spots = []
    for slot in range(slots):
        t = slot if slots > 1 else jnp.where(owners[1] >> 1 == here >> 1, 1, 0)
        own = owners[t] == here
        both = jnp.concatenate(halves_of(listed, t, core), axis=1)
        spots.append(chosen(both, lines.shape[0], own))
    spots = jnp.concatenate(spots, axis=1)
    for at in range(CHUNKS):
        columns = slice(at * chunk, (at + 1) * chunk)
        loads[at].wait()
        value = lax.dot_general(
            spots, lines[:, columns], (((0,), (0,)), ((), ())), preferred_element_type=jnp.float32
        ).astype(kept.dtype)
        value = value.reshape(slots, 2, plane, each, chunk)
        for slot in range(slots):
            kept[:, slot, :, columns] = value[slot, 0]
            sent[:, slot, :, columns] = value[slot, 1]


def targets_kernel(device, owners, batch_rows, targets, kept, sent, *, sizes):
    here = device[0]
    core = here & (sizes[3] - 1)
    half = batch_rows.shape[1] // 2
    for t in range(ITERS):
        own = owners[t] == here
        for rows, out in zip(halves_of(batch_rows, t, core), (kept, sent)):
            out[:, t * half : (t + 1) * half] = jnp.dot(
                targets[...],
                chosen(rows, targets.shape[1], own),
                preferred_element_type=jnp.float32,
            ).astype(out.dtype)


def pick_kernel(device, owners, scattered, piece, *, sizes):
    _, z, _, _ = place(device[0], sizes)
    slots = scattered.shape[1]
    for t in range(ITERS):
        root_y, root_z, root_x, _ = place(owners[t], sizes)
        block = scattered[root_y * sizes[2] + root_x, t if slots > 1 else 0]
        piece[t] = jnp.where(root_z == z, block, jnp.zeros_like(block))


def along_kernel(device, owners, scattered, out, *, sizes):
    _, z, _, _ = place(device[0], sizes)
    t = jnp.where(place(owners[1], sizes)[1] == z, 1, 0)
    root_y, _, root_x, _ = place(owners[t], sizes)
    out[...] = jnp.broadcast_to(scattered[root_y * sizes[2] + root_x, 0][None], out.shape)


def arrived_kernel(owners, along, piece, *, sizes):
    for t in range(ITERS):
        piece[t] = along[place(owners[t], sizes)[1]]


def spread_kernel(piece, out):
    out[...] = jnp.broadcast_to(piece[...][None], out.shape)


def tile_kernel(batch, own, other, own_norms, other_norms, tile, *, each, factor):
    lines = batch[...]
    norms = jnp.sqrt(
        jnp.sum(jnp.square(lines.astype(jnp.float32)), axis=1, keepdims=True) + EPSILON
    )
    count = lines.shape[0] // ITERS
    width = own.shape[0]
    for at, (centers, center_norms) in enumerate(((own, own_norms), (other, other_norms))):
        dots = lax.dot_general(lines, centers[...], NT, preferred_element_type=jnp.float32)
        scaled = dots / (norms * center_norms[...]) * factor
        value = scaled + scaled * scaled * scaled / 3.0
        value = value.reshape(count // each, ITERS, each, width)
        for t in range(ITERS):
            tile[t, :, at * width : (at + 1) * width] = (
                value[:, t].reshape(count, width).astype(tile.dtype)
            )


def partial_kernel(core, tile, came, own, other, kept, arrived, lines, *, root_scale):
    outs, width = own.shape
    count = tile.shape[1]
    step = aligned(outs)
    lines[...] = jnp.zeros_like(lines)
    held = kept[...].astype(jnp.float32) + arrived[...].astype(jnp.float32)
    for t in range(ITERS):
        total = lax.dot_general(
            own[...],
            tile[t, :, :width].astype(jnp.float32),
            NT,
            precision=HIGHEST,
            preferred_element_type=jnp.float32,
        ) + lax.dot_general(
            other[...],
            tile[t, :, width:].astype(jnp.float32),
            NT,
            precision=HIGHEST,
            preferred_element_type=jnp.float32,
        )
        lines[t * step : t * step + outs, :] = (
            total / root_scale - held[:, t * count : (t + 1) * count]
        )
    mine = tile[0]
    theirs = jnp.concatenate([came[0, :, width:], came[0, :, :width]], axis=1)
    later = tile[1]
    gram = [
        lax.dot_general(value, later, NT, preferred_element_type=jnp.float32)
        for value in (mine, theirs)
    ]
    is_first = core[0] == 0
    lines[2 * step : 2 * step + count, :] = jnp.where(is_first, gram[0], gram[1])
    lines[2 * step + count : 2 * step + 2 * count, :] = jnp.where(is_first, gram[1], gram[0])


def finish_kernel(core, mine, other, tile, came, coefficients, trained, residuals, *, total):
    outs, width = coefficients.shape
    count = mine.shape[1]
    step = aligned(outs)
    is_first = core[0] == 0

    def both(start, size):
        kept, sent = mine[start : start + size, :], other[start : start + size, :]
        return jnp.concatenate(
            [jnp.where(is_first, kept, sent), jnp.where(is_first, sent, kept)], axis=1
        )

    first = both(0, outs)
    gram = both(2 * step, 2 * count)
    second = both(step, outs) - STEP_RATE / total * jnp.dot(
        first, gram, precision=HIGHEST, preferred_element_type=jnp.float32
    )
    update = None
    for t, residual in enumerate((first, second)):
        residuals[:, t, :] = residual
        kept = tile[t, :, :width].astype(jnp.float32)
        sent = came[t, :, width:].astype(jnp.float32)
        rows = jnp.concatenate(
            [jnp.where(is_first, kept, sent), jnp.where(is_first, sent, kept)], axis=0
        )
        term = jnp.dot(residual, rows, precision=HIGHEST, preferred_element_type=jnp.float32)
        update = term if update is None else update + term
    trained[...] = coefficients[...] - STEP_RATE / math.sqrt(total) * update


def call(kernel, out_shape, operands, scalars=0, out_kinds=None, in_place=(), scratch=()):
    outs = out_shape if isinstance(out_shape, tuple) else (out_shape,)
    out_kinds = out_kinds or [pltpu.VMEM] * len(outs)
    specs = tuple(pl.BlockSpec(memory_space=kind) for kind in out_kinds)
    kinds = [pltpu.SMEM] * scalars + [pltpu.VMEM] * (len(operands) - scalars)
    kinds = [pltpu.HBM if at in in_place else kind for at, kind in enumerate(kinds)]
    operands = [
        value if kind is pltpu.SMEM else pltpu.with_memory_space_constraint(value, kind)
        for value, kind in zip(operands, kinds)
    ]
    return pl.pallas_call(
        kernel,
        in_specs=[pl.BlockSpec(memory_space=kind) for kind in kinds],
        out_specs=specs if isinstance(out_shape, tuple) else specs[0],
        out_shape=out_shape,
        scratch_shapes=scratch,
        compiler_params=pltpu.CompilerParams(vmem_limit_bytes=SCRATCH),
    )(*operands)


def body(spectra, targets, centers, coefficients, owners, batch_rows):
    width, features = centers.shape
    outs = coefficients.shape[1]
    batch = batch_rows.shape[1]
    half = batch // 2
    total = width * lax.axis_size(AXES)
    sizes = tuple(lax.axis_size(name) for name in AXES)
    plane = sizes[0] * sizes[2]
    each = half // plane
    device = lax.axis_index(AXES).reshape(1)
    core = lax.axis_index("core").reshape(1)
    narrow = jnp.bfloat16
    block = pltpu.VMEM((ITERS, each, features), narrow)

    def rows_for(slots):
        blocks = pltpu.VMEM((plane, slots, each, features), narrow)
        flag = (jax.ShapeDtypeStruct((1,), jnp.int32),) if slots == 1 else ()
        return call(
            functools.partial(rows_kernel, sizes=sizes),
            (blocks, blocks) + flag,
            (device, owners, batch_rows, spectra),
            scalars=2,
            out_kinds=[pltpu.VMEM, pltpu.VMEM] + [pltpu.SMEM] * len(flag),
            in_place=(2, 3),
            scratch=(
                pltpu.VMEM(spectra.shape, narrow),
                pltpu.VMEM(batch_rows.shape, jnp.int32),
                pltpu.SemaphoreType.DMA((CHUNKS + 1,)),
            ),
        )

    def in_steps(kept, sent):
        piece = call(
            functools.partial(pick_kernel, sizes=sizes),
            block,
            (device, owners, exchange(kept + swap(sent), PLANE)),
            scalars=2,
        )
        for mask in Z_MASKS:
            piece = piece + lax.ppermute(piece, "z", [(i, i ^ mask) for i in range(sizes[1])])
        return piece

    def at_once(kept, sent):
        along = call(
            functools.partial(along_kernel, sizes=sizes),
            pltpu.VMEM((sizes[1], each, features), narrow),
            (device, owners, exchange(kept + swap(sent), PLANE)),
            scalars=2,
        )
        return call(
            functools.partial(arrived_kernel, sizes=sizes),
            block,
            (owners, exchange(along, "z")),
            scalars=1,
        )

    kept, sent, apart = rows_for(1)
    piece = lax.switch(
        apart[0],
        (lambda: in_steps(*rows_for(2)), lambda: in_steps(kept, sent), lambda: at_once(kept, sent)),
    )
    spread_out = call(
        spread_kernel, pltpu.VMEM((plane, ITERS, each, features), narrow), (piece,)
    )
    gathered = exchange(spread_out, PLANE).reshape(ITERS * half, features)

    shown = pltpu.VMEM((outs, ITERS * half), narrow)
    kept_targets, sent_targets = call(
        functools.partial(targets_kernel, sizes=sizes),
        (shown, shown),
        (device, owners, batch_rows, targets.T),
        scalars=2,
    )
    came_targets = swap(sent_targets)

    turned = coefficients.T
    turned_other = swap(turned)
    other_centers = swap(centers)
    norms = [jnp.sqrt(squares(value) + EPSILON).reshape(1, -1) for value in (centers, other_centers)]

    tile = call(
        functools.partial(tile_kernel, each=each, factor=math.sqrt(features)),
        pltpu.VMEM((ITERS, half, 2 * width), narrow),
        (gathered, centers, other_centers, *norms),
    )
    came = swap(tile)
    height = -(-(2 * aligned(outs) + batch) // (8 * plane)) * 8
    lines = call(
        functools.partial(partial_kernel, root_scale=math.sqrt(total)),
        pltpu.VMEM((plane * height, half), jnp.float32),
        (core, tile, came, turned, turned_other, kept_targets, came_targets),
        scalars=1,
    )
    own = exchange(lines.reshape(plane, height, half), PLANE).sum(axis=0)
    own = copies(own, "z").sum(axis=0)
    whole = copies(own, PLANE).reshape(plane * height, half)
    trained, residuals = call(
        functools.partial(finish_kernel, total=total),
        (
            jax.ShapeDtypeStruct((outs, width), jnp.float32),
            jax.ShapeDtypeStruct((outs, ITERS, batch), jnp.float32),
        ),
        (core, whole, swap(whole), tile, came, turned),
        scalars=1,
    )
    return trained.T, jnp.transpose(residuals, (1, 2, 0))


def solution(mesh):
    torus = Mesh(mesh.devices.reshape(4, 8, 4, 2), AXES)
    return jax.shard_map(
        body,
        mesh=torus,
        in_specs=(P(AXES, None), P(AXES, None), P(AXES, None), P(AXES, None), P(), P()),
        out_specs=(P(AXES, None), P()),
        check_vma=False,
    )
```

```python
import functools
import math

import jax
import jax.numpy as jnp
from jax import lax
from jax.experimental import pallas as pl
from jax.experimental.pallas import tpu as pltpu
from jax.sharding import Mesh
from jax.sharding import PartitionSpec as P

ITERS = 2
AXES = ("y", "z", "x", "core")
PLANE = ("y", "x")
EPSILON = 1e-06
STEP_RATE = 0.2
SCRATCH = 16 << 20
CHUNKS = 4
GROUP = 4
HIGHEST = lax.Precision.HIGHEST
NT = (((1,), (1,)), ((), ()))


def exchange(blocks, axes):
    return lax.all_to_all(blocks, axes, 0, 0, tiled=True)


def place(device, sizes):
    bits = [size.bit_length() - 1 for size in sizes]
    core = device & (sizes[3] - 1)
    x = device >> bits[3] & (sizes[2] - 1)
    z = device >> (bits[3] + bits[2]) & (sizes[1] - 1)
    return device >> (bits[3] + bits[2] + bits[1]), z, x, core


def chosen(rows, held, own):
    spots = lax.broadcasted_iota(jnp.int32, (held, rows.shape[1]), 0) == rows
    return jnp.where(spots & own, 1.0, 0.0).astype(jnp.bfloat16)


def halves_of(batch_rows, t, core):
    rows = batch_rows[pl.ds(t, 1), :] if not isinstance(t, int) else batch_rows[t : t + 1, :]
    half = rows.shape[1] // 2
    first, second = rows[:, :half], rows[:, half:]
    return jnp.where(core == 0, first, second), jnp.where(core == 0, second, first)


def copies(value, axes):
    size = lax.axis_size(axes)
    return exchange(jnp.broadcast_to(value[None], (size, *value.shape)), axes)


def squares(value):
    return jnp.sum(jnp.square(value.astype(jnp.float32)), axis=1)


def aligned(size):
    return -(-size // 8) * 8


def rows_kernel(device, owners, batch_rows, spectra, kept, sent, *rest, sizes):
    flag, (lines, listed, arrivals) = rest[:-3], rest[-3:]
    here = device[0]
    core = here & (sizes[3] - 1)
    plane, slots, each, features = kept.shape
    chunk = features // CHUNKS
    listing = pltpu.make_async_copy(batch_rows, listed, arrivals.at[CHUNKS])
    listing.start()
    loads = []
    for at in range(CHUNKS):
        columns = slice(at * chunk, (at + 1) * chunk)
        load = pltpu.make_async_copy(spectra.at[:, columns], lines.at[:, columns], arrivals.at[at])
        load.start()
        loads.append(load)
    if flag:
        flag[0][0] = jnp.where(owners[0] >> 1 == owners[1] >> 1, 0, 1)
    listing.wait()
    spots = []
    for slot in range(slots):
        t = slot if slots > 1 else jnp.where(owners[1] >> 1 == here >> 1, 1, 0)
        own = owners[t] == here
        both = jnp.concatenate(halves_of(listed, t, core), axis=1)
        spots.append(chosen(both, lines.shape[0], own))
    spots = jnp.concatenate(spots, axis=1)
    for at in range(CHUNKS):
        columns = slice(at * chunk, (at + 1) * chunk)
        loads[at].wait()
        value = lax.dot_general(
            spots, lines[:, columns], (((0,), (0,)), ((), ())), preferred_element_type=jnp.float32
        ).astype(kept.dtype)
        value = value.reshape(slots, 2, plane, each, chunk)
        for slot in range(slots):
            kept[:, slot, :, columns] = value[slot, 0]
            sent[:, slot, :, columns] = value[slot, 1]


def targets_kernel(device, owners, batch_rows, targets, near, across, *, sizes):
    here = device[0]
    core = here & (sizes[3] - 1)
    batch_of = place(here, sizes)[1] & 1
    half = batch_rows.shape[1] // 2
    for t, out in ((batch_of, near), (1 - batch_of, across)):
        for at, rows in enumerate(halves_of(batch_rows, t, core)):
            out[:, at * half : (at + 1) * half] = jnp.dot(
                targets[...],
                chosen(rows, targets.shape[1], owners[t] == here),
                preferred_element_type=jnp.float32,
            ).astype(out.dtype)


def along_kernel(owners, scattered, out, *, sizes):
    slots = scattered.shape[1]
    for t in range(ITERS):
        root_y, _, root_x, _ = place(owners[t], sizes)
        block = scattered[root_y * sizes[2] + root_x, t if slots > 1 else 0]
        for z in range(t, sizes[1], ITERS):
            out[z] = block


def spread_kernel(device, owners, along, out, *, sizes):
    t = place(device[0], sizes)[1] & 1
    out[...] = jnp.broadcast_to(along[place(owners[t], sizes)[1]][None], out.shape)


def tile_kernel(member, batch, *rest, factor):
    centers, norms, (tile, turned) = rest[:GROUP], rest[GROUP : 2 * GROUP], rest[2 * GROUP :]
    lines = batch[...]
    lengths = jnp.sqrt(
        jnp.sum(jnp.square(lines.astype(jnp.float32)), axis=1, keepdims=True) + EPSILON
    )
    for at in range(GROUP):
        dots = lax.dot_general(lines, centers[at][...], NT, preferred_element_type=jnp.float32)
        scaled = dots / (lengths * norms[at][...]) * factor
        value = (scaled + scaled * scaled * scaled / 3.0).astype(tile.dtype)
        turned[at] = value
        tile[member[0] ^ at] = value


def partial_kernel(turned, *rest, root_scale):
    coefficients, (near, came, lines) = rest[:GROUP], rest[GROUP:]
    outs = lines.shape[0]
    total = None
    for at in range(GROUP):
        term = lax.dot_general(
            coefficients[at][...],
            turned[at].astype(jnp.float32),
            NT,
            precision=HIGHEST,
            preferred_element_type=jnp.float32,
        )
        total = term if total is None else total + term
    held = near[...].astype(jnp.float32) + came[...].astype(jnp.float32)
    lines[...] = total / root_scale - held


def join_kernel(member, partial, tile, came, lines):
    outs, count = partial.shape
    step = aligned(outs)
    first = member[0] < 2
    gram = None
    for at in range(GROUP):
        mine, theirs = tile[at], came[at]
        term = lax.dot_general(
            jnp.where(first, mine, theirs),
            jnp.where(first, theirs, mine),
            NT,
            preferred_element_type=jnp.float32,
        )
        gram = term if gram is None else gram + term
    lines[:outs] = partial[...]
    lines[outs:step] = jnp.zeros((step - outs, count), jnp.float32)
    lines[step : step + count] = gram
    lines[step + count :] = jnp.zeros((lines.shape[0] - step - count, count), jnp.float32)


def finish_kernel(member, mine, other, *rest, total):
    tiles, (coefficients, trained, residuals, kept) = rest[:GROUP], rest[GROUP:]
    outs, _ = coefficients.shape
    blocks, _, height, count = mine.shape
    step = aligned(outs)
    is_first = member[0] & 1 == 0

    def lines_of(t):
        own = mine[:, t].reshape(blocks * height, count)
        sent = other[:, t].reshape(blocks * height, count)
        return jnp.where(is_first, own, sent), jnp.where(is_first, sent, own)

    early, late = lines_of(0), lines_of(1)
    quarters = [value[step : step + count] for value in (*early, *late)]
    gram = jnp.concatenate(
        [
            jnp.concatenate([quarters[0], quarters[3]], axis=1),
            jnp.concatenate([quarters[2], quarters[1]], axis=1),
        ],
        axis=0,
    )
    first = jnp.concatenate([value[:outs] for value in early], axis=1)
    second = jnp.concatenate([value[:outs] for value in late], axis=1)
    second = second - STEP_RATE / total * jnp.dot(
        first, gram, precision=HIGHEST, preferred_element_type=jnp.float32
    )
    for t, residual in enumerate((first, second)):
        residuals[:, t, :] = residual
        for at in range(2):
            kept[2 * t + at] = residual[:, at * count : (at + 1) * count]
    update = None
    for at in range(GROUP):
        term = jnp.dot(
            kept[member[0] ^ at],
            tiles[at][...].astype(jnp.float32),
            precision=HIGHEST,
            preferred_element_type=jnp.float32,
        )
        update = term if update is None else update + term
    trained[...] = coefficients[...] - STEP_RATE / math.sqrt(total) * update


def call(kernel, out_shape, operands, scalars=0, out_kinds=None, in_place=(), scratch=()):
    outs = out_shape if isinstance(out_shape, tuple) else (out_shape,)
    out_kinds = out_kinds or [pltpu.VMEM] * len(outs)
    specs = tuple(pl.BlockSpec(memory_space=kind) for kind in out_kinds)
    kinds = [pltpu.SMEM] * scalars + [pltpu.VMEM] * (len(operands) - scalars)
    kinds = [pltpu.HBM if at in in_place else kind for at, kind in enumerate(kinds)]
    operands = [
        value if kind is pltpu.SMEM else pltpu.with_memory_space_constraint(value, kind)
        for value, kind in zip(operands, kinds)
    ]
    return pl.pallas_call(
        kernel,
        in_specs=[pl.BlockSpec(memory_space=kind) for kind in kinds],
        out_specs=specs if isinstance(out_shape, tuple) else specs[0],
        out_shape=out_shape,
        scratch_shapes=scratch,
        compiler_params=pltpu.CompilerParams(vmem_limit_bytes=SCRATCH),
    )(*operands)


def body(spectra, targets, centers, coefficients, owners, batch_rows):
    width, features = centers.shape
    outs = coefficients.shape[1]
    batch = batch_rows.shape[1]
    half = batch // 2
    total = width * lax.axis_size(AXES)
    sizes = tuple(lax.axis_size(name) for name in AXES)
    plane = sizes[0] * sizes[2]
    each = half // plane
    device = lax.axis_index(AXES).reshape(1)
    narrow = jnp.bfloat16
    z_size, core_size = sizes[1], sizes[3]
    member = ((lax.axis_index("z") & 1) * core_size + lax.axis_index("core")).reshape(1)

    def move(value, target):
        pairs = []
        for z in range(z_size):
            for c in range(core_size):
                to = target((z & 1) * core_size + c)
                pairs.append((z * core_size + c, (z - (z & 1) + to // 2) * core_size + to % 2))
        return lax.ppermute(value, ("z", "core"), pairs)

    def by(value, mask):
        return move(value, lambda at: at ^ mask)

    def rows_for(slots):
        blocks = pltpu.VMEM((plane, slots, each, features), narrow)
        flag = (jax.ShapeDtypeStruct((1,), jnp.int32),) if slots == 1 else ()
        return call(
            functools.partial(rows_kernel, sizes=sizes),
            (blocks, blocks) + flag,
            (device, owners, batch_rows, spectra),
            scalars=2,
            out_kinds=[pltpu.VMEM, pltpu.VMEM] + [pltpu.SMEM] * len(flag),
            in_place=(2, 3),
            scratch=(
                pltpu.VMEM(spectra.shape, narrow),
                pltpu.VMEM(batch_rows.shape, jnp.int32),
                pltpu.SemaphoreType.DMA((CHUNKS + 1,)),
            ),
        )

    def scatter(kept, sent):
        return call(
            functools.partial(along_kernel, sizes=sizes),
            pltpu.VMEM((z_size, each, features), narrow),
            (owners, exchange(kept + by(sent, 1), PLANE)),
            scalars=1,
        )

    kept, sent, apart = rows_for(1)
    along = lax.cond(apart[0] != 0, lambda: scatter(kept, sent), lambda: scatter(*rows_for(2)))
    spread_out = call(
        functools.partial(spread_kernel, sizes=sizes),
        pltpu.VMEM((plane, each, features), narrow),
        (device, owners, exchange(along, "z")),
        scalars=2,
    )
    gathered = exchange(spread_out, PLANE).reshape(half, features)

    shown = pltpu.VMEM((outs, batch), narrow)
    near, across = call(
        functools.partial(targets_kernel, sizes=sizes),
        (shown, shown),
        (device, owners, batch_rows, targets.T),
        scalars=2,
    )
    near = near + by(across, 2)
    came_targets = by(near[:, half:], 1)

    turned = coefficients.T
    both_centers = [centers, by(centers, 2)]
    both_coefficients = [turned, by(turned, 2)]
    all_centers = [both_centers[0], by(both_centers[0], 1), both_centers[1], by(both_centers[1], 1)]
    all_coefficients = [
        both_coefficients[0],
        by(both_coefficients[0], 1),
        both_coefficients[1],
        by(both_coefficients[1], 1),
    ]
    norms = [jnp.sqrt(squares(value) + EPSILON).reshape(1, -1) for value in all_centers]

    square = pltpu.VMEM((GROUP, half, width), narrow)
    tile, turned_tile = call(
        functools.partial(tile_kernel, factor=math.sqrt(features)),
        (square, square),
        (member, gathered, *all_centers, *norms),
        scalars=1,
    )
    came = move(tile, lambda at: at ^ 2 if at >= 2 else at ^ 3)
    partial = call(
        functools.partial(partial_kernel, root_scale=math.sqrt(total)),
        pltpu.VMEM((outs, half), jnp.float32),
        (turned_tile, *all_coefficients, near[:, :half], came_targets),
    )
    height = -(-(aligned(outs) + half) // (8 * plane)) * 8
    lines = call(
        join_kernel,
        pltpu.VMEM((plane * height, half), jnp.float32),
        (member, partial, tile, came),
        scalars=1,
    )
    tiles = [turned_tile[0]] + [by(turned_tile[at], at) for at in range(1, GROUP)]
    own = exchange(lines.reshape(plane, height, half), PLANE).sum(axis=0)
    own = copies(own, "z").reshape(z_size // 2, 2, height, half).sum(axis=0)
    whole = copies(own, PLANE)
    trained, residuals = call(
        functools.partial(finish_kernel, total=total),
        (
            jax.ShapeDtypeStruct((outs, width), jnp.float32),
            jax.ShapeDtypeStruct((outs, ITERS, batch), jnp.float32),
        ),
        (member, whole, by(whole, 1), *tiles, turned),
        scalars=1,
        scratch=(pltpu.VMEM((GROUP, outs, half), jnp.float32),),
    )
    return trained.T, jnp.transpose(residuals, (1, 2, 0))


def solution(mesh):
    torus = Mesh(mesh.devices.reshape(4, 8, 4, 2), AXES)
    return jax.shard_map(
        body,
        mesh=torus,
        in_specs=(P(AXES, None), P(AXES, None), P(AXES, None), P(AXES, None), P(), P()),
        out_specs=(P(AXES, None), P()),
        check_vma=False,
    )
```

```python
import functools
import math

import jax
import jax.numpy as jnp
from jax import lax
from jax.experimental import pallas as pl
from jax.experimental.pallas import tpu as pltpu
from jax.sharding import Mesh
from jax.sharding import PartitionSpec as P

ITERS = 2
AXES = ("y", "z", "x", "core")
PLANE = ("y", "x")
EPSILON = 1e-06
STEP_RATE = 0.2
SCRATCH = 16 << 20
CHUNKS = 4
GROUP = 4
HIGHEST = lax.Precision.HIGHEST
NT = (((1,), (1,)), ((), ()))


def exchange(blocks, axes):
    return lax.all_to_all(blocks, axes, 0, 0, tiled=True)


def place(device, sizes):
    bits = [size.bit_length() - 1 for size in sizes]
    core = device & (sizes[3] - 1)
    x = device >> bits[3] & (sizes[2] - 1)
    z = device >> (bits[3] + bits[2]) & (sizes[1] - 1)
    return device >> (bits[3] + bits[2] + bits[1]), z, x, core


def chosen(rows, held, own):
    spots = lax.broadcasted_iota(jnp.int32, (held, rows.shape[1]), 0) == rows
    return jnp.where(spots & own, 1.0, 0.0).astype(jnp.bfloat16)


def halves_of(batch_rows, t, core):
    rows = batch_rows[pl.ds(t, 1), :] if not isinstance(t, int) else batch_rows[t : t + 1, :]
    half = rows.shape[1] // 2
    first, second = rows[:, :half], rows[:, half:]
    return jnp.where(core == 0, first, second), jnp.where(core == 0, second, first)


def copies(value, axes):
    size = lax.axis_size(axes)
    return exchange(jnp.broadcast_to(value[None], (size, *value.shape)), axes)


def squares(value):
    return jnp.sum(jnp.square(value.astype(jnp.float32)), axis=1)


def aligned(size):
    return -(-size // 8) * 8


def rows_kernel(device, owners, batch_rows, spectra, kept, sent, *rest, sizes):
    flag, (lines, listed, arrivals) = rest[:-3], rest[-3:]
    here = device[0]
    core = here & (sizes[3] - 1)
    plane, slots, each, features = kept.shape
    chunk = features // CHUNKS
    listing = pltpu.make_async_copy(batch_rows, listed, arrivals.at[CHUNKS])
    listing.start()
    loads = []
    for at in range(CHUNKS):
        columns = slice(at * chunk, (at + 1) * chunk)
        load = pltpu.make_async_copy(spectra.at[:, columns], lines.at[:, columns], arrivals.at[at])
        load.start()
        loads.append(load)
    if flag:
        flag[0][0] = jnp.where(owners[0] >> 1 == owners[1] >> 1, 0, 1)
    listing.wait()
    spots = []
    for slot in range(slots):
        t = slot if slots > 1 else jnp.where(owners[1] >> 1 == here >> 1, 1, 0)
        own = owners[t] == here
        both = jnp.concatenate(halves_of(listed, t, core), axis=1)
        spots.append(chosen(both, lines.shape[0], own))
    spots = jnp.concatenate(spots, axis=1)
    for at in range(CHUNKS):
        columns = slice(at * chunk, (at + 1) * chunk)
        loads[at].wait()
        value = lax.dot_general(
            spots, lines[:, columns], (((0,), (0,)), ((), ())), preferred_element_type=jnp.float32
        ).astype(kept.dtype)
        value = value.reshape(slots, 2, plane, each, chunk)
        for slot in range(slots):
            kept[:, slot, :, columns] = value[slot, 0]
            sent[:, slot, :, columns] = value[slot, 1]


def targets_kernel(device, owners, batch_rows, targets, near, across, *, sizes):
    here = device[0]
    core = here & (sizes[3] - 1)
    batch_of = place(here, sizes)[1] & 1
    half = batch_rows.shape[1] // 2
    for t, out in ((batch_of, near), (1 - batch_of, across)):
        for at, rows in enumerate(halves_of(batch_rows, t, core)):
            out[:, at * half : (at + 1) * half] = jnp.dot(
                targets[...],
                chosen(rows, targets.shape[1], owners[t] == here),
                preferred_element_type=jnp.float32,
            ).astype(out.dtype)


def along_kernel(owners, scattered, out, *, sizes):
    slots = scattered.shape[1]
    for t in range(ITERS):
        root_y, _, root_x, _ = place(owners[t], sizes)
        block = scattered[root_y * sizes[2] + root_x, t if slots > 1 else 0]
        for z in range(t, sizes[1], ITERS):
            out[z] = block


def spread_kernel(device, owners, along, out, *, sizes):
    t = place(device[0], sizes)[1] & 1
    out[...] = jnp.broadcast_to(along[place(owners[t], sizes)[1]][None], out.shape)


def tile_kernel(member, batch, *rest, factor):
    centers, norms, (tile, turned) = rest[:GROUP], rest[GROUP : 2 * GROUP], rest[2 * GROUP :]
    lines = batch[...]
    lengths = jnp.sqrt(
        jnp.sum(jnp.square(lines.astype(jnp.float32)), axis=1, keepdims=True) + EPSILON
    )
    for at in range(GROUP):
        dots = lax.dot_general(lines, centers[at][...], NT, preferred_element_type=jnp.float32)
        scaled = dots / (lengths * norms[at][...]) * factor
        value = (scaled + scaled * scaled * scaled / 3.0).astype(tile.dtype)
        turned[at] = value
        tile[member[0] ^ at] = value


def partial_kernel(turned, *rest, root_scale):
    coefficients, (near, came, lines) = rest[:GROUP], rest[GROUP:]
    outs = lines.shape[0]
    total = None
    for at in range(GROUP):
        term = lax.dot_general(
            coefficients[at][...],
            turned[at].astype(jnp.float32),
            NT,
            precision=HIGHEST,
            preferred_element_type=jnp.float32,
        )
        total = term if total is None else total + term
    held = near[...].astype(jnp.float32) + came[...].astype(jnp.float32)
    lines[...] = total / root_scale - held


def join_kernel(member, partial, tile, came, lines):
    outs, count = partial.shape
    step = aligned(outs)
    first = member[0] < 2
    gram = None
    for at in range(GROUP):
        mine, theirs = tile[at], came[at]
        term = lax.dot_general(
            jnp.where(first, mine, theirs),
            jnp.where(first, theirs, mine),
            NT,
            preferred_element_type=jnp.float32,
        )
        gram = term if gram is None else gram + term
    lines[:outs] = partial[...]
    lines[outs:step] = jnp.zeros((step - outs, count), jnp.float32)
    lines[step : step + count] = gram
    lines[step + count :] = jnp.zeros((lines.shape[0] - step - count, count), jnp.float32)


def finish_kernel(member, mine, other, *rest, total):
    tiles, (coefficients, trained, residuals, kept) = rest[:GROUP], rest[GROUP:]
    outs, _ = coefficients.shape
    blocks, _, height, count = mine.shape
    step = aligned(outs)
    is_first = member[0] & 1 == 0

    def lines_of(t):
        own = mine[:, t].reshape(blocks * height, count)
        sent = other[:, t].reshape(blocks * height, count)
        return jnp.where(is_first, own, sent), jnp.where(is_first, sent, own)

    early, late = lines_of(0), lines_of(1)
    quarters = [value[step : step + count] for value in (*early, *late)]
    gram = jnp.concatenate(
        [
            jnp.concatenate([quarters[0], quarters[3]], axis=1),
            jnp.concatenate([quarters[2], quarters[1]], axis=1),
        ],
        axis=0,
    )
    first = jnp.concatenate([value[:outs] for value in early], axis=1)
    second = jnp.concatenate([value[:outs] for value in late], axis=1)
    second = second - STEP_RATE / total * jnp.dot(
        first, gram, precision=HIGHEST, preferred_element_type=jnp.float32
    )
    for t, residual in enumerate((first, second)):
        residuals[:, t, :] = residual
        for at in range(2):
            kept[2 * t + at] = residual[:, at * count : (at + 1) * count]
    update = None
    for at in range(GROUP):
        term = jnp.dot(
            kept[member[0] ^ at],
            tiles[at][...].astype(jnp.float32),
            precision=HIGHEST,
            preferred_element_type=jnp.float32,
        )
        update = term if update is None else update + term
    trained[...] = coefficients[...] - STEP_RATE / math.sqrt(total) * update


def call(kernel, out_shape, operands, scalars=0, out_kinds=None, in_place=(), scratch=()):
    outs = out_shape if isinstance(out_shape, tuple) else (out_shape,)
    out_kinds = out_kinds or [pltpu.VMEM] * len(outs)
    specs = tuple(pl.BlockSpec(memory_space=kind) for kind in out_kinds)
    kinds = [pltpu.SMEM] * scalars + [pltpu.VMEM] * (len(operands) - scalars)
    kinds = [pltpu.HBM if at in in_place else kind for at, kind in enumerate(kinds)]
    operands = [
        value if kind is pltpu.SMEM else pltpu.with_memory_space_constraint(value, kind)
        for value, kind in zip(operands, kinds)
    ]
    return pl.pallas_call(
        kernel,
        in_specs=[pl.BlockSpec(memory_space=kind) for kind in kinds],
        out_specs=specs if isinstance(out_shape, tuple) else specs[0],
        out_shape=out_shape,
        scratch_shapes=scratch,
        compiler_params=pltpu.CompilerParams(vmem_limit_bytes=SCRATCH),
    )(*operands)


def body(spectra, targets, centers, coefficients, owners, batch_rows):
    width, features = centers.shape
    outs = coefficients.shape[1]
    batch = batch_rows.shape[1]
    half = batch // 2
    total = width * lax.axis_size(AXES)
    sizes = tuple(lax.axis_size(name) for name in AXES)
    plane = sizes[0] * sizes[2]
    each = half // plane
    device = lax.axis_index(AXES).reshape(1)
    narrow = jnp.bfloat16
    z_size, core_size = sizes[1], sizes[3]
    member = ((lax.axis_index("z") & 1) * core_size + lax.axis_index("core")).reshape(1)

    def move(value, target):
        pairs = []
        for z in range(z_size):
            for c in range(core_size):
                to = target((z & 1) * core_size + c)
                pairs.append((z * core_size + c, (z - (z & 1) + to // 2) * core_size + to % 2))
        return lax.ppermute(value, ("z", "core"), pairs)

    def by(value, mask):
        return move(value, lambda at: at ^ mask)

    def rows_for(slots):
        blocks = pltpu.VMEM((plane, slots, each, features), narrow)
        flag = (jax.ShapeDtypeStruct((1,), jnp.int32),) if slots == 1 else ()
        return call(
            functools.partial(rows_kernel, sizes=sizes),
            (blocks, blocks) + flag,
            (device, owners, batch_rows, spectra),
            scalars=2,
            out_kinds=[pltpu.VMEM, pltpu.VMEM] + [pltpu.SMEM] * len(flag),
            in_place=(2, 3),
            scratch=(
                pltpu.VMEM(spectra.shape, narrow),
                pltpu.VMEM(batch_rows.shape, jnp.int32),
                pltpu.SemaphoreType.DMA((CHUNKS + 1,)),
            ),
        )

    def scatter(kept, sent):
        return call(
            functools.partial(along_kernel, sizes=sizes),
            pltpu.VMEM((z_size, each, features), narrow),
            (owners, exchange(kept + by(sent, 1), PLANE)),
            scalars=1,
        )

    def reach(kept, sent):
        return exchange(scatter(kept, sent), "z")

    kept, sent, apart = rows_for(1)
    along = lax.cond(apart[0] != 0, lambda: reach(kept, sent), lambda: reach(*rows_for(2)))
    spread_out = call(
        functools.partial(spread_kernel, sizes=sizes),
        pltpu.VMEM((plane, each, features), narrow),
        (device, owners, along),
        scalars=2,
    )
    gathered = exchange(spread_out, PLANE).reshape(half, features)

    shown = pltpu.VMEM((outs, batch), narrow)
    near, across = call(
        functools.partial(targets_kernel, sizes=sizes),
        (shown, shown),
        (device, owners, batch_rows, targets.T),
        scalars=2,
    )
    near = near + by(across, 2)
    came_targets = by(near[:, half:], 1)

    turned = coefficients.T
    both_centers = [centers, by(centers, 2)]
    both_coefficients = [turned, by(turned, 2)]
    all_centers = [both_centers[0], by(both_centers[0], 1), both_centers[1], by(both_centers[1], 1)]
    all_coefficients = [
        both_coefficients[0],
        by(both_coefficients[0], 1),
        both_coefficients[1],
        by(both_coefficients[1], 1),
    ]
    norms = [jnp.sqrt(squares(value) + EPSILON).reshape(1, -1) for value in all_centers]

    gathered, all_centers, all_coefficients, near, came_targets, norms = lax.optimization_barrier(
        (gathered, all_centers, all_coefficients, near, came_targets, norms)
    )
    square = pltpu.VMEM((GROUP, half, width), narrow)
    tile, turned_tile = call(
        functools.partial(tile_kernel, factor=math.sqrt(features)),
        (square, square),
        (member, gathered, *all_centers, *norms),
        scalars=1,
    )
    came = move(tile, lambda at: at ^ 2 if at >= 2 else at ^ 3)
    partial = call(
        functools.partial(partial_kernel, root_scale=math.sqrt(total)),
        pltpu.VMEM((outs, half), jnp.float32),
        (turned_tile, *all_coefficients, near[:, :half], came_targets),
    )
    height = -(-(aligned(outs) + half) // (8 * plane)) * 8
    lines = call(
        join_kernel,
        pltpu.VMEM((plane * height, half), jnp.float32),
        (member, partial, tile, came),
        scalars=1,
    )
    tiles = [turned_tile[0]] + [by(turned_tile[at], at) for at in range(1, GROUP)]
    own = exchange(lines.reshape(plane, height, half), PLANE).sum(axis=0)
    own, tiles = lax.optimization_barrier((own, tiles))
    own = copies(own, "z").reshape(z_size // 2, 2, height, half).sum(axis=0)
    whole = copies(own, PLANE)
    trained, residuals = call(
        functools.partial(finish_kernel, total=total),
        (
            jax.ShapeDtypeStruct((outs, width), jnp.float32),
            jax.ShapeDtypeStruct((outs, ITERS, batch), jnp.float32),
        ),
        (member, whole, by(whole, 1), *tiles, turned),
        scalars=1,
        scratch=(pltpu.VMEM((GROUP, outs, half), jnp.float32),),
    )
    return trained.T, jnp.transpose(residuals, (1, 2, 0))


def solution(mesh):
    torus = Mesh(mesh.devices.reshape(4, 8, 4, 2), AXES)
    return jax.shard_map(
        body,
        mesh=torus,
        in_specs=(P(AXES, None), P(AXES, None), P(AXES, None), P(AXES, None), P(), P()),
        out_specs=(P(AXES, None), P()),
        check_vma=False,
    )
```

```python
import functools
import math

import jax
import jax.numpy as jnp
from jax import lax
from jax.experimental import pallas as pl
from jax.experimental.pallas import tpu as pltpu
from jax.sharding import Mesh
from jax.sharding import PartitionSpec as P

ITERS = 2
AXES = ("y", "z", "x", "core")
PLANE = ("y", "x")
EPSILON = 1e-06
STEP_RATE = 0.2
PAIR = [(0, 1), (1, 0)]
Z_MASKS = (1, 2, 7)
SCRATCH = 16 << 20
CHUNKS = 4
HIGHEST = lax.Precision.HIGHEST
NT = (((1,), (1,)), ((), ()))
NN = (((1,), (0,)), ((), ()))


def swap(value):
    return lax.ppermute(value, "core", PAIR)


def exchange(blocks, axes):
    return lax.all_to_all(blocks, axes, 0, 0, tiled=True)


def place(device, sizes):
    bits = [size.bit_length() - 1 for size in sizes]
    core = device & (sizes[3] - 1)
    x = device >> bits[3] & (sizes[2] - 1)
    z = device >> (bits[3] + bits[2]) & (sizes[1] - 1)
    return device >> (bits[3] + bits[2] + bits[1]), z, x, core


def chosen(rows, held, own):
    spots = lax.broadcasted_iota(jnp.int32, (held, rows.shape[1]), 0) == rows
    return jnp.where(spots & own, 1.0, 0.0).astype(jnp.bfloat16)


def halves_of(batch_rows, t, core):
    rows = batch_rows[pl.ds(t, 1), :] if not isinstance(t, int) else batch_rows[t : t + 1, :]
    half = rows.shape[1] // 2
    first, second = rows[:, :half], rows[:, half:]
    return jnp.where(core == 0, first, second), jnp.where(core == 0, second, first)


def copies(value, axes):
    size = lax.axis_size(axes)
    return exchange(jnp.broadcast_to(value[None], (size, *value.shape)), axes)


def squares(value):
    return jnp.sum(jnp.square(value.astype(jnp.float32)), axis=1)


def aligned(size):
    return -(-size // 8) * 8


def rows_kernel(device, owners, batch_rows, spectra, kept, sent, *rest, sizes):
    flag, (lines, listed, arrivals) = rest[:-3], rest[-3:]
    here = device[0]
    core = here & (sizes[3] - 1)
    plane, slots, each, features = kept.shape
    chunk = features // CHUNKS
    later = owners[1] >> 1 == here >> 1
    involved = later | (owners[0] >> 1 == here >> 1)
    if flag:
        same_chip = owners[0] >> 1 == owners[1] >> 1
        same_z = place(owners[0], sizes)[1] == place(owners[1], sizes)[1]
        flag[0][0] = jnp.where(same_chip, 0, jnp.where(same_z, 1, 2))

    @pl.when(jnp.logical_not(involved))
    def _():
        kept[...] = jnp.zeros_like(kept)
        sent[...] = jnp.zeros_like(sent)

    @pl.when(involved)
    def _():
        listing = pltpu.make_async_copy(batch_rows, listed, arrivals.at[CHUNKS])
        listing.start()
        loads = []
        for at in range(CHUNKS):
            columns = slice(at * chunk, (at + 1) * chunk)
            load = pltpu.make_async_copy(
                spectra.at[:, columns], lines.at[:, columns], arrivals.at[at]
            )
            load.start()
            loads.append(load)
        listing.wait()
        spots = []
        for slot in range(slots):
            t = slot if slots > 1 else jnp.where(later, 1, 0)
            both = jnp.concatenate(halves_of(listed, t, core), axis=1)
            spots.append(chosen(both, lines.shape[0], owners[t] == here))
        spots = jnp.concatenate(spots, axis=1)
        for at in range(CHUNKS):
            columns = slice(at * chunk, (at + 1) * chunk)
            loads[at].wait()
            value = lax.dot_general(
                spots,
                lines[:, columns],
                (((0,), (0,)), ((), ())),
                preferred_element_type=jnp.float32,
            ).astype(kept.dtype)
            value = value.reshape(slots, 2, plane, each, chunk)
            for slot in range(slots):
                kept[:, slot, :, columns] = value[slot, 0]
                sent[:, slot, :, columns] = value[slot, 1]


def targets_kernel(device, owners, batch_rows, targets, kept, sent, *, sizes):
    here = device[0]
    core = here & (sizes[3] - 1)
    half = batch_rows.shape[1] // 2
    for t in range(ITERS):
        own = owners[t] == here
        for rows, out in zip(halves_of(batch_rows, t, core), (kept, sent)):
            out[:, t * half : (t + 1) * half] = jnp.dot(
                targets[...],
                chosen(rows, targets.shape[1], own),
                preferred_element_type=jnp.float32,
            ).astype(out.dtype)


def pick_kernel(device, owners, scattered, piece, *, sizes):
    _, z, _, _ = place(device[0], sizes)
    slots = scattered.shape[1]
    for t in range(ITERS):
        root_y, root_z, root_x, _ = place(owners[t], sizes)
        block = scattered[root_y * sizes[2] + root_x, t if slots > 1 else 0]
        piece[t] = jnp.where(root_z == z, block, jnp.zeros_like(block))


def along_kernel(device, owners, scattered, out, *, sizes):
    _, z, _, _ = place(device[0], sizes)
    t = jnp.where(place(owners[1], sizes)[1] == z, 1, 0)
    root_y, _, root_x, _ = place(owners[t], sizes)
    out[...] = jnp.broadcast_to(scattered[root_y * sizes[2] + root_x, 0][None], out.shape)


def spread_kernel(owners, along, out, *, sizes):
    plane, _, each, features = out.shape
    for t in range(ITERS):
        block = along[place(owners[t], sizes)[1]]
        out[:, t] = jnp.broadcast_to(block[None], (plane, each, features))


def spread_steps_kernel(piece, arrived, out):
    out[...] = jnp.broadcast_to((piece[...] + arrived[...])[None], out.shape)


def pieces_of(value):
    pieces = []
    for _ in range(3):
        piece = value.astype(jnp.bfloat16)
        pieces.append(piece)
        value = value - piece.astype(jnp.float32)
    return pieces


def wide_dot(pieces, value, dims):
    total = None
    for piece in reversed(pieces):
        term = lax.dot_general(piece, value, dims, preferred_element_type=jnp.float32)
        total = term if total is None else total + term
    return total


def tile_kernel(batch, own, other, own_norms, other_norms, tile, *, each, factor):
    lines = batch[...]
    norms = jnp.sqrt(
        jnp.sum(jnp.square(lines.astype(jnp.float32)), axis=1, keepdims=True) + EPSILON
    )
    count = lines.shape[0] // ITERS
    width = own.shape[0]
    for at, (centers, center_norms) in enumerate(((own, own_norms), (other, other_norms))):
        dots = lax.dot_general(lines, centers[...], NT, preferred_element_type=jnp.float32)
        scaled = dots / (norms * center_norms[...]) * factor
        value = scaled + scaled * scaled * scaled / 3.0
        value = value.reshape(count // each, ITERS, each, width)
        for t in range(ITERS):
            tile[t, :, at * width : (at + 1) * width] = (
                value[:, t].reshape(count, width).astype(tile.dtype)
            )


def partial_kernel(core, tile, came, own, other, kept, arrived, lines, *, root_scale):
    outs, width = own.shape
    count = tile.shape[1]
    step = aligned(outs)
    lines[...] = jnp.zeros_like(lines)
    held = kept[...].astype(jnp.float32) + arrived[...].astype(jnp.float32)
    own_pieces, other_pieces = pieces_of(own[...]), pieces_of(other[...])
    for t in range(ITERS):
        total = wide_dot(own_pieces, tile[t, :, :width], NT) + wide_dot(
            other_pieces, tile[t, :, width:], NT
        )
        lines[t * step : t * step + outs, :] = (
            total / root_scale - held[:, t * count : (t + 1) * count]
        )
    mine = tile[0]
    theirs = jnp.concatenate([came[0, :, width:], came[0, :, :width]], axis=1)
    later = tile[1]
    gram = [
        lax.dot_general(value, later, NT, preferred_element_type=jnp.float32)
        for value in (mine, theirs)
    ]
    is_first = core[0] == 0
    lines[2 * step : 2 * step + count, :] = jnp.where(is_first, gram[0], gram[1])
    lines[2 * step + count : 2 * step + 2 * count, :] = jnp.where(is_first, gram[1], gram[0])


def finish_kernel(core, mine, other, tile, came, coefficients, trained, residuals, *, total):
    outs, width = coefficients.shape
    count = mine.shape[1]
    step = aligned(outs)
    is_first = core[0] == 0

    def both(start, size):
        kept, sent = mine[start : start + size, :], other[start : start + size, :]
        return jnp.concatenate(
            [jnp.where(is_first, kept, sent), jnp.where(is_first, sent, kept)], axis=1
        )

    first = both(0, outs)
    gram = both(2 * step, 2 * count)
    second = both(step, outs) - STEP_RATE / total * jnp.dot(
        first, gram, precision=HIGHEST, preferred_element_type=jnp.float32
    )
    update = None
    for t, residual in enumerate((first, second)):
        residuals[:, t, :] = residual
        kept, sent = tile[t, :, :width], came[t, :, width:]
        rows = jnp.concatenate(
            [jnp.where(is_first, kept, sent), jnp.where(is_first, sent, kept)], axis=0
        )
        term = wide_dot(pieces_of(residual), rows, NN)
        update = term if update is None else update + term
    trained[...] = coefficients[...] - STEP_RATE / math.sqrt(total) * update


def call(kernel, out_shape, operands, scalars=0, out_kinds=None, in_place=(), scratch=()):
    outs = out_shape if isinstance(out_shape, tuple) else (out_shape,)
    out_kinds = out_kinds or [pltpu.VMEM] * len(outs)
    specs = tuple(pl.BlockSpec(memory_space=kind) for kind in out_kinds)
    kinds = [pltpu.SMEM] * scalars + [pltpu.VMEM] * (len(operands) - scalars)
    kinds = [pltpu.HBM if at in in_place else kind for at, kind in enumerate(kinds)]
    operands = [
        value if kind is pltpu.SMEM else pltpu.with_memory_space_constraint(value, kind)
        for value, kind in zip(operands, kinds)
    ]
    return pl.pallas_call(
        kernel,
        in_specs=[pl.BlockSpec(memory_space=kind) for kind in kinds],
        out_specs=specs if isinstance(out_shape, tuple) else specs[0],
        out_shape=out_shape,
        scratch_shapes=scratch,
        compiler_params=pltpu.CompilerParams(vmem_limit_bytes=SCRATCH),
    )(*operands)


def body(spectra, targets, centers, coefficients, owners, batch_rows):
    width, features = centers.shape
    outs = coefficients.shape[1]
    batch = batch_rows.shape[1]
    half = batch // 2
    total = width * lax.axis_size(AXES)
    sizes = tuple(lax.axis_size(name) for name in AXES)
    plane = sizes[0] * sizes[2]
    each = half // plane
    device = lax.axis_index(AXES).reshape(1)
    core = lax.axis_index("core").reshape(1)
    narrow = jnp.bfloat16
    block = pltpu.VMEM((ITERS, each, features), narrow)
    whole_block = jax.ShapeDtypeStruct((plane, ITERS, each, features), narrow)

    def rows_for(slots):
        blocks = pltpu.VMEM((plane, slots, each, features), narrow)
        flag = (pltpu.SMEM((1,), jnp.int32),) if slots == 1 else ()
        return call(
            functools.partial(rows_kernel, sizes=sizes),
            (blocks, blocks) + flag,
            (device, owners, batch_rows, spectra),
            scalars=2,
            out_kinds=[pltpu.VMEM, pltpu.VMEM] + [pltpu.SMEM] * len(flag),
            in_place=(2, 3),
            scratch=(
                pltpu.VMEM(spectra.shape, narrow),
                pltpu.VMEM(batch_rows.shape, jnp.int32),
                pltpu.SemaphoreType.DMA((CHUNKS + 1,)),
            ),
        )

    def in_steps(kept, sent):
        piece = call(
            functools.partial(pick_kernel, sizes=sizes),
            block,
            (device, owners, exchange(kept + swap(sent), PLANE)),
            scalars=2,
        )
        arrived = None
        for mask in Z_MASKS:
            piece = piece if arrived is None else piece + arrived
            arrived = lax.ppermute(piece, "z", [(i, i ^ mask) for i in range(sizes[1])])
        return call(spread_steps_kernel, whole_block, (piece, arrived))

    def at_once(kept, sent):
        along = call(
            functools.partial(along_kernel, sizes=sizes),
            pltpu.VMEM((sizes[1], each, features), narrow),
            (device, owners, exchange(kept + swap(sent), PLANE)),
            scalars=2,
        )
        return call(
            functools.partial(spread_kernel, sizes=sizes),
            whole_block,
            (owners, exchange(along, "z")),
            scalars=1,
        )

    kept, sent, apart = rows_for(1)
    spread_out = lax.switch(
        apart[0],
        (lambda: in_steps(*rows_for(2)), lambda: in_steps(kept, sent), lambda: at_once(kept, sent)),
    )
    gathered = exchange(spread_out, PLANE).reshape(ITERS * half, features)

    shown = pltpu.VMEM((outs, ITERS * half), narrow)
    kept_targets, sent_targets = call(
        functools.partial(targets_kernel, sizes=sizes),
        (shown, shown),
        (device, owners, batch_rows, targets.T),
        scalars=2,
    )
    came_targets = swap(sent_targets)

    turned = coefficients.T
    turned_other = swap(turned)
    other_centers = swap(centers)
    norms = [jnp.sqrt(squares(value) + EPSILON).reshape(1, -1) for value in (centers, other_centers)]

    tile = call(
        functools.partial(tile_kernel, each=each, factor=math.sqrt(features)),
        pltpu.VMEM((ITERS, half, 2 * width), narrow),
        (gathered, centers, other_centers, *norms),
    )
    came = swap(tile)
    height = -(-(2 * aligned(outs) + batch) // (8 * plane)) * 8
    lines = call(
        functools.partial(partial_kernel, root_scale=math.sqrt(total)),
        pltpu.VMEM((plane * height, half), jnp.float32),
        (core, tile, came, turned, turned_other, kept_targets, came_targets),
        scalars=1,
    )
    own = exchange(lines.reshape(plane, height, half), PLANE).sum(axis=0)
    own = copies(own, "z").sum(axis=0)
    whole = copies(own, PLANE).reshape(plane * height, half)
    trained, residuals = call(
        functools.partial(finish_kernel, total=total),
        (
            jax.ShapeDtypeStruct((outs, width), jnp.float32),
            jax.ShapeDtypeStruct((outs, ITERS, batch), jnp.float32),
        ),
        (core, whole, swap(whole), tile, came, turned),
        scalars=1,
    )
    return trained.T, jnp.transpose(residuals, (1, 2, 0))


def solution(mesh):
    torus = Mesh(mesh.devices.reshape(4, 8, 4, 2), AXES)
    return jax.shard_map(
        body,
        mesh=torus,
        in_specs=(P(AXES, None), P(AXES, None), P(AXES, None), P(AXES, None), P(), P()),
        out_specs=(P(AXES, None), P()),
        check_vma=False,
    )
```

```python
import functools
import math

import jax
import jax.numpy as jnp
from jax import lax
from jax.experimental import pallas as pl
from jax.experimental.pallas import tpu as pltpu
from jax.sharding import Mesh
from jax.sharding import PartitionSpec as P

ITERS = 2
AXES = ("y", "z", "x", "core")
PLANE = ("y", "x")
EPSILON = 1e-06
STEP_RATE = 0.2
SCRATCH = 16 << 20
CHUNKS = 4
GROUP = 4
HIGHEST = lax.Precision.HIGHEST
NT = (((1,), (1,)), ((), ()))
NN = (((1,), (0,)), ((), ()))


def exchange(blocks, axes):
    return lax.all_to_all(blocks, axes, 0, 0, tiled=True)


def place(device, sizes):
    bits = [size.bit_length() - 1 for size in sizes]
    core = device & (sizes[3] - 1)
    x = device >> bits[3] & (sizes[2] - 1)
    z = device >> (bits[3] + bits[2]) & (sizes[1] - 1)
    return device >> (bits[3] + bits[2] + bits[1]), z, x, core


def chosen(rows, held, own):
    spots = lax.broadcasted_iota(jnp.int32, (held, rows.shape[1]), 0) == rows
    return jnp.where(spots & own, 1.0, 0.0).astype(jnp.bfloat16)


def halves_of(batch_rows, t, core):
    rows = batch_rows[pl.ds(t, 1), :] if not isinstance(t, int) else batch_rows[t : t + 1, :]
    half = rows.shape[1] // 2
    first, second = rows[:, :half], rows[:, half:]
    return jnp.where(core == 0, first, second), jnp.where(core == 0, second, first)


def copies(value, axes):
    size = lax.axis_size(axes)
    return exchange(jnp.broadcast_to(value[None], (size, *value.shape)), axes)


def squares(value):
    return jnp.sum(jnp.square(value.astype(jnp.float32)), axis=1)


def aligned(size):
    return -(-size // 8) * 8


def rows_kernel(device, owners, batch_rows, spectra, targets, kept, sent, *rest, sizes):
    extra, (lines, shown, listed, arrivals) = rest[:-4], rest[-4:]
    here = device[0]
    core = here & (sizes[3] - 1)
    plane, slots, each, features = kept.shape
    chunk = features // CHUNKS
    later = owners[1] >> 1 == here >> 1
    involved = later | (owners[0] >> 1 == here >> 1)
    if extra:
        near, across, flag = extra
        flag[0] = jnp.where(owners[0] >> 1 == owners[1] >> 1, 0, 1)

    @pl.when(jnp.logical_not(involved))
    def _():
        kept[...] = jnp.zeros_like(kept)
        sent[...] = jnp.zeros_like(sent)
        for out in extra[:2]:
            out[...] = jnp.zeros_like(out)

    @pl.when(involved)
    def _():
        listing = pltpu.make_async_copy(batch_rows, listed, arrivals.at[CHUNKS])
        listing.start()
        loads = []
        for at in range(CHUNKS):
            columns = slice(at * chunk, (at + 1) * chunk)
            load = pltpu.make_async_copy(
                spectra.at[:, columns], lines.at[:, columns], arrivals.at[at]
            )
            load.start()
            loads.append(load)
        if extra:
            showing = pltpu.make_async_copy(targets, shown, arrivals.at[CHUNKS + 1])
            showing.start()
        listing.wait()
        spots = []
        for slot in range(slots):
            t = slot if slots > 1 else jnp.where(later, 1, 0)
            both = jnp.concatenate(halves_of(listed, t, core), axis=1)
            spots.append(chosen(both, lines.shape[0], owners[t] == here))
        spots = jnp.concatenate(spots, axis=1)
        for at in range(CHUNKS):
            columns = slice(at * chunk, (at + 1) * chunk)
            loads[at].wait()
            value = lax.dot_general(
                spots,
                lines[:, columns],
                (((0,), (0,)), ((), ())),
                preferred_element_type=jnp.float32,
            ).astype(kept.dtype)
            value = value.reshape(slots, 2, plane, each, chunk)
            for slot in range(slots):
                kept[:, slot, :, columns] = value[slot, 0]
                sent[:, slot, :, columns] = value[slot, 1]
        if extra:
            showing.wait()
            batch_of = place(here, sizes)[1] & 1
            for t, out in ((batch_of, near), (1 - batch_of, across)):
                both = jnp.concatenate(halves_of(listed, t, core), axis=1)
                out[...] = jnp.dot(
                    shown[...],
                    chosen(both, lines.shape[0], owners[t] == here),
                    preferred_element_type=jnp.float32,
                ).astype(out.dtype)


def along_kernel(owners, scattered, out, *, sizes):
    slots = scattered.shape[1]
    for t in range(ITERS):
        root_y, _, root_x, _ = place(owners[t], sizes)
        block = scattered[root_y * sizes[2] + root_x, t if slots > 1 else 0]
        for z in range(t, sizes[1], ITERS):
            out[z] = block


def spread_kernel(device, owners, along, out, *, sizes):
    t = place(device[0], sizes)[1] & 1
    out[...] = jnp.broadcast_to(along[place(owners[t], sizes)[1]][None], out.shape)


def pieces_of(value):
    pieces = []
    for _ in range(3):
        piece = value.astype(jnp.bfloat16)
        pieces.append(piece)
        value = value - piece.astype(jnp.float32)
    return pieces


def wide_dot(pieces, value, dims):
    total = None
    for piece in reversed(pieces):
        term = lax.dot_general(piece, value, dims, preferred_element_type=jnp.float32)
        total = term if total is None else total + term
    return total


def tile_kernel(member, batch, *rest, factor):
    centers, norms, (tile, turned, side) = rest[:GROUP], rest[GROUP : 2 * GROUP], rest[2 * GROUP :]
    lines = batch[...]
    lengths = jnp.sqrt(
        jnp.sum(jnp.square(lines.astype(jnp.float32)), axis=1, keepdims=True) + EPSILON
    )
    for at in range(GROUP):
        dots = lax.dot_general(lines, centers[at][...], NT, preferred_element_type=jnp.float32)
        scaled = dots / (lengths * norms[at][...]) * factor
        value = (scaled + scaled * scaled * scaled / 3.0).astype(tile.dtype)
        turned[at] = value
        tile[member[0] ^ at] = value
    side[...] = jnp.where(member[0] < 2, turned[2], turned[3])


def partial_kernel(turned, *rest, root_scale):
    coefficients, (near, came, lines) = rest[:GROUP], rest[GROUP:]
    outs = lines.shape[0]
    total = None
    for at in range(GROUP):
        term = wide_dot(pieces_of(coefficients[at][...]), turned[at], NT)
        total = term if total is None else total + term
    held = near[...].astype(jnp.float32) + came[...].astype(jnp.float32)
    lines[...] = total / root_scale - held


def join_kernel(member, partial, tile, came, lines):
    outs, count = partial.shape
    step = aligned(outs)
    first = member[0] < 2
    gram = None
    for at in range(GROUP):
        mine, theirs = tile[at], came[at]
        term = lax.dot_general(
            jnp.where(first, mine, theirs),
            jnp.where(first, theirs, mine),
            NT,
            preferred_element_type=jnp.float32,
        )
        gram = term if gram is None else gram + term
    lines[:outs] = partial[...]
    lines[outs:step] = jnp.zeros((step - outs, count), jnp.float32)
    lines[step : step + count] = gram
    lines[step + count :] = jnp.zeros((lines.shape[0] - step - count, count), jnp.float32)


def finish_kernel(
    member, mine, other, tile, came, paired, beside, coefficients, trained, residuals, kept, *, total
):
    outs, _ = coefficients.shape
    blocks, _, height, count = mine.shape
    step = aligned(outs)
    is_first = member[0] & 1 == 0

    def lines_of(t):
        own = mine[:, t].reshape(blocks * height, count)
        sent = other[:, t].reshape(blocks * height, count)
        return jnp.where(is_first, own, sent), jnp.where(is_first, sent, own)

    early, late = lines_of(0), lines_of(1)
    quarters = [value[step : step + count] for value in (*early, *late)]
    gram = jnp.concatenate(
        [
            jnp.concatenate([quarters[0], quarters[3]], axis=1),
            jnp.concatenate([quarters[2], quarters[1]], axis=1),
        ],
        axis=0,
    )
    first = jnp.concatenate([value[:outs] for value in early], axis=1)
    second = jnp.concatenate([value[:outs] for value in late], axis=1)
    second = second - STEP_RATE / total * jnp.dot(
        first, gram, precision=HIGHEST, preferred_element_type=jnp.float32
    )
    for t, residual in enumerate((first, second)):
        residuals[:, t, :] = residual
        for at in range(2):
            kept[2 * t + at] = residual[:, at * count : (at + 1) * count]
    given, even = came[member[0]], member[0] < 2
    tiles = (
        tile[0],
        paired[...],
        jnp.where(even, given, beside[...]),
        jnp.where(even, beside[...], given),
    )
    update = None
    for at in range(GROUP):
        term = wide_dot(pieces_of(kept[member[0] ^ at]), tiles[at], NN)
        update = term if update is None else update + term
    trained[...] = coefficients[...] - STEP_RATE / math.sqrt(total) * update


def call(kernel, out_shape, operands, scalars=0, out_kinds=None, in_place=(), scratch=()):
    outs = out_shape if isinstance(out_shape, tuple) else (out_shape,)
    out_kinds = out_kinds or [pltpu.VMEM] * len(outs)
    specs = tuple(pl.BlockSpec(memory_space=kind) for kind in out_kinds)
    kinds = [pltpu.SMEM] * scalars + [pltpu.VMEM] * (len(operands) - scalars)
    kinds = [pltpu.HBM if at in in_place else kind for at, kind in enumerate(kinds)]
    operands = [
        value if kind is pltpu.SMEM else pltpu.with_memory_space_constraint(value, kind)
        for value, kind in zip(operands, kinds)
    ]
    return pl.pallas_call(
        kernel,
        in_specs=[pl.BlockSpec(memory_space=kind) for kind in kinds],
        out_specs=specs if isinstance(out_shape, tuple) else specs[0],
        out_shape=out_shape,
        scratch_shapes=scratch,
        compiler_params=pltpu.CompilerParams(vmem_limit_bytes=SCRATCH),
    )(*operands)


def body(spectra, targets, centers, coefficients, owners, batch_rows):
    width, features = centers.shape
    outs = coefficients.shape[1]
    batch = batch_rows.shape[1]
    half = batch // 2
    total = width * lax.axis_size(AXES)
    sizes = tuple(lax.axis_size(name) for name in AXES)
    plane = sizes[0] * sizes[2]
    each = half // plane
    device = lax.axis_index(AXES).reshape(1)
    narrow = jnp.bfloat16
    z_size, core_size = sizes[1], sizes[3]
    member = ((lax.axis_index("z") & 1) * core_size + lax.axis_index("core")).reshape(1)

    def move(value, target):
        pairs = []
        for z in range(z_size):
            for c in range(core_size):
                to = target((z & 1) * core_size + c)
                pairs.append((z * core_size + c, (z - (z & 1) + to // 2) * core_size + to % 2))
        return lax.ppermute(value, ("z", "core"), pairs)

    def by(value, mask):
        return move(value, lambda at: at ^ mask)

    turned = coefficients.T
    shown = pltpu.VMEM((outs, batch), narrow)

    def rows_for(slots):
        blocks = pltpu.VMEM((plane, slots, each, features), narrow)
        extra = (shown, shown, pltpu.SMEM((1,), jnp.int32)) if slots == 1 else ()
        return call(
            functools.partial(rows_kernel, sizes=sizes),
            (blocks, blocks) + extra,
            (device, owners, batch_rows, spectra, targets.T),
            scalars=2,
            out_kinds=[pltpu.VMEM] * (2 + len(extra[:2])) + [pltpu.SMEM] * len(extra[2:]),
            in_place=(2, 3, 4),
            scratch=(
                pltpu.VMEM(spectra.shape, narrow),
                pltpu.VMEM(targets.shape[::-1], narrow),
                pltpu.VMEM(batch_rows.shape, jnp.int32),
                pltpu.SemaphoreType.DMA((CHUNKS + 2,)),
            ),
        )

    def scatter(kept, sent):
        return call(
            functools.partial(along_kernel, sizes=sizes),
            pltpu.VMEM((z_size, each, features), narrow),
            (owners, exchange(kept + by(sent, 1), PLANE)),
            scalars=1,
        )

    def reach(kept, sent):
        return exchange(scatter(kept, sent), "z")

    kept, sent, near, across, apart = rows_for(1)
    along = lax.cond(apart[0] != 0, lambda: reach(kept, sent), lambda: reach(*rows_for(2)))
    spread_out = call(
        functools.partial(spread_kernel, sizes=sizes),
        pltpu.VMEM((plane, each, features), narrow),
        (device, owners, along),
        scalars=2,
    )
    near = near + by(across, 2)
    near, turned, spread_out = lax.optimization_barrier((near, turned, spread_out))
    came_targets = by(near[:, half:], 1)
    gathered = exchange(spread_out, PLANE).reshape(half, features)

    both_centers = [centers, by(centers, 2)]
    both_coefficients = [turned, by(turned, 2)]
    all_centers = [both_centers[0], by(both_centers[0], 1), both_centers[1], by(both_centers[1], 1)]
    all_coefficients = [
        both_coefficients[0],
        by(both_coefficients[0], 1),
        both_coefficients[1],
        by(both_coefficients[1], 1),
    ]
    norms = [jnp.sqrt(squares(value) + EPSILON).reshape(1, -1) for value in all_centers]

    gathered, all_centers, all_coefficients, near, came_targets, norms = lax.optimization_barrier(
        (gathered, all_centers, all_coefficients, near, came_targets, norms)
    )
    square = pltpu.VMEM((GROUP, half, width), narrow)
    tile, turned_tile, side = call(
        functools.partial(tile_kernel, factor=math.sqrt(features)),
        (square, square, pltpu.VMEM((half, width), narrow)),
        (member, gathered, *all_centers, *norms),
        scalars=1,
    )
    came = move(tile, lambda at: at ^ 2 if at >= 2 else at ^ 3)
    partial = call(
        functools.partial(partial_kernel, root_scale=math.sqrt(total)),
        pltpu.VMEM((outs, half), jnp.float32),
        (turned_tile, *all_coefficients, near[:, :half], came_targets),
    )
    height = -(-(aligned(outs) + half) // (8 * plane)) * 8
    lines = call(
        join_kernel,
        pltpu.VMEM((plane * height, half), jnp.float32),
        (member, partial, tile, came),
        scalars=1,
    )
    paired = by(turned_tile[1], 1)
    beside = move(side, lambda at: at ^ 2 if at < 2 else at ^ 3)
    lines, paired, beside = lax.optimization_barrier((lines, paired, beside))
    own = exchange(lines.reshape(plane, height, half), PLANE).sum(axis=0)
    own = copies(own, "z").reshape(z_size // 2, 2, height, half).sum(axis=0)
    whole = copies(own, PLANE)
    trained, residuals = call(
        functools.partial(finish_kernel, total=total),
        (
            jax.ShapeDtypeStruct((outs, width), jnp.float32),
            jax.ShapeDtypeStruct((outs, ITERS, batch), jnp.float32),
        ),
        (member, whole, by(whole, 1), turned_tile, came, paired, beside, turned),
        scalars=1,
        scratch=(pltpu.VMEM((GROUP, outs, half), jnp.float32),),
    )
    return trained.T, jnp.transpose(residuals, (1, 2, 0))


def solution(mesh):
    torus = Mesh(mesh.devices.reshape(4, 8, 4, 2), AXES)
    return jax.shard_map(
        body,
        mesh=torus,
        in_specs=(P(AXES, None), P(AXES, None), P(AXES, None), P(AXES, None), P(), P()),
        out_specs=(P(AXES, None), P()),
        check_vma=False,
    )
```

```python
import functools
import math

import jax
import jax.numpy as jnp
from jax import lax
from jax.experimental import pallas as pl
from jax.experimental.pallas import tpu as pltpu
from jax.sharding import Mesh
from jax.sharding import PartitionSpec as P


ITERS = 2
AXES = ("y", "z", "x", "core")
PLANE = ("y", "x")
EPSILON = 1e-06
STEP_RATE = 0.2
SCRATCH = 16 << 20
CHUNKS = 4
GROUP = 4
HIGHEST = lax.Precision.HIGHEST
NT = (((1,), (1,)), ((), ()))
NN = (((1,), (0,)), ((), ()))


def exchange(blocks, axes):
    return lax.all_to_all(blocks, axes, 0, 0, tiled=True)


def place(device, sizes):
    bits = [size.bit_length() - 1 for size in sizes]
    core = device & (sizes[3] - 1)
    x = device >> bits[3] & (sizes[2] - 1)
    z = device >> (bits[3] + bits[2]) & (sizes[1] - 1)
    return device >> (bits[3] + bits[2] + bits[1]), z, x, core


def chosen(rows, held, own):
    spots = lax.broadcasted_iota(jnp.int32, (held, rows.shape[1]), 0) == rows
    return jnp.where(spots & own, 1.0, 0.0).astype(jnp.bfloat16)


def halves_of(batch_rows, t, core):
    rows = batch_rows[pl.ds(t, 1), :] if not isinstance(t, int) else batch_rows[t : t + 1, :]
    half = rows.shape[1] // 2
    first, second = rows[:, :half], rows[:, half:]
    return jnp.where(core == 0, first, second), jnp.where(core == 0, second, first)


def copies(value, axes):
    size = lax.axis_size(axes)
    return exchange(jnp.broadcast_to(value[None], (size, *value.shape)), axes)


def squares(value):
    return jnp.sum(jnp.square(value.astype(jnp.float32)), axis=1)


def aligned(size):
    return -(-size // 8) * 8


def rows_kernel(device, owners, batch_rows, spectra, targets, kept, sent, *rest, sizes):
    extra, (lines, shown, listed, arrivals) = rest[:-4], rest[-4:]
    here = device[0]
    core = here & (sizes[3] - 1)
    plane, slots, each, features = kept.shape
    chunk = features // CHUNKS
    later = owners[1] >> 1 == here >> 1
    involved = later | (owners[0] >> 1 == here >> 1)
    if extra:
        near, across, flag = extra
        flag[0] = jnp.where(owners[0] >> 1 == owners[1] >> 1, 0, 1)

    @pl.when(jnp.logical_not(involved))
    def _():
        for out in extra[:2]:
            out[...] = jnp.zeros_like(out)

    @pl.when(involved)
    def _():
        listing = pltpu.make_async_copy(batch_rows, listed, arrivals.at[CHUNKS])
        listing.start()
        loads = []
        for at in range(CHUNKS):
            columns = slice(at * chunk, (at + 1) * chunk)
            load = pltpu.make_async_copy(
                spectra.at[:, columns], lines.at[:, columns], arrivals.at[at]
            )
            load.start()
            loads.append(load)
        if extra:
            showing = pltpu.make_async_copy(targets, shown, arrivals.at[CHUNKS + 1])
            showing.start()
        listing.wait()
        spots = []
        for slot in range(slots):
            t = slot if slots > 1 else jnp.where(later, 1, 0)
            both = jnp.concatenate(halves_of(listed, t, core), axis=1)
            spots.append(chosen(both, lines.shape[0], owners[t] == here))
        spots = jnp.concatenate(spots, axis=1)
        for at in range(CHUNKS):
            columns = slice(at * chunk, (at + 1) * chunk)
            loads[at].wait()
            value = lax.dot_general(
                spots,
                lines[:, columns],
                (((0,), (0,)), ((), ())),
                preferred_element_type=jnp.float32,
            ).astype(kept.dtype)
            value = value.reshape(slots, 2, plane, each, chunk)
            for slot in range(slots):
                kept[:, slot, :, columns] = value[slot, 0]
                sent[:, slot, :, columns] = value[slot, 1]
        if extra:
            showing.wait()
            batch_of = place(here, sizes)[1] & 1
            for t, out in ((batch_of, near), (1 - batch_of, across)):
                both = jnp.concatenate(halves_of(listed, t, core), axis=1)
                out[...] = jnp.dot(
                    shown[...],
                    chosen(both, lines.shape[0], owners[t] == here),
                    preferred_element_type=jnp.float32,
                ).astype(out.dtype)


def along_kernel(owners, scattered, out, *, sizes):
    slots = scattered.shape[1]
    for t in range(ITERS):
        root_y, _, root_x, _ = place(owners[t], sizes)
        block = scattered[root_y * sizes[2] + root_x, t if slots > 1 else 0]
        for z in range(t, sizes[1], ITERS):
            out[z] = block


def spread_kernel(device, owners, along, out, *, sizes):
    t = place(device[0], sizes)[1] & 1
    out[...] = jnp.broadcast_to(along[place(owners[t], sizes)[1]][None], out.shape)


def pieces_of(value):
    pieces = []
    for _ in range(3):
        piece = value.astype(jnp.bfloat16)
        pieces.append(piece)
        value = value - piece.astype(jnp.float32)
    return pieces


def wide_dot(pieces, value, dims):
    total = None
    for piece in reversed(pieces):
        term = lax.dot_general(piece, value, dims, preferred_element_type=jnp.float32)
        total = term if total is None else total + term
    return total


def tile_kernel(member, batch, *rest, factor):
    centers, norms, (tile, turned, side) = rest[:GROUP], rest[GROUP : 2 * GROUP], rest[2 * GROUP :]
    lines = batch[...]
    lengths = jnp.sqrt(
        jnp.sum(jnp.square(lines.astype(jnp.float32)), axis=1, keepdims=True) + EPSILON
    )
    for at in range(GROUP):
        dots = lax.dot_general(lines, centers[at][...], NT, preferred_element_type=jnp.float32)
        scaled = dots / (lengths * norms[at][...]) * factor
        value = (scaled + scaled * scaled * scaled / 3.0).astype(tile.dtype)
        turned[at] = value
        tile[member[0] ^ at] = value
    side[...] = jnp.where(member[0] < 2, turned[2], turned[3])


def partial_kernel(turned, *rest, root_scale):
    coefficients, (near, came, lines) = rest[:GROUP], rest[GROUP:]
    total = None
    for at in range(GROUP):
        term = wide_dot(pieces_of(coefficients[at][...]), turned[at], NT)
        total = term if total is None else total + term
    held = near[...].astype(jnp.float32) + came[...].astype(jnp.float32)
    lines[...] = total / root_scale - held


def join_kernel(member, partial, tile, came, lines):
    outs, count = partial.shape
    step = aligned(outs)
    first = member[0] < 2
    gram = None
    for at in range(GROUP):
        mine, theirs = tile[at], came[at]
        term = lax.dot_general(
            jnp.where(first, mine, theirs),
            jnp.where(first, theirs, mine),
            NT,
            preferred_element_type=jnp.float32,
        )
        gram = term if gram is None else gram + term
    lines[:outs] = partial[...]
    lines[outs:step] = jnp.zeros((step - outs, count), jnp.float32)
    lines[step : step + count] = gram
    lines[step + count :] = jnp.zeros((lines.shape[0] - step - count, count), jnp.float32)


def finish_kernel(
    member, mine, other, tile, came, paired, beside, coefficients, trained, residuals, tiles, *, total
):
    outs, _ = coefficients.shape
    blocks, _, height, count = mine.shape
    step = aligned(outs)
    is_first = member[0] & 1 == 0

    def lines_of(t):
        own = mine[:, t].reshape(blocks * height, count)
        sent = other[:, t].reshape(blocks * height, count)
        return jnp.where(is_first, own, sent), jnp.where(is_first, sent, own)

    early, late = lines_of(0), lines_of(1)
    quarters = [value[step : step + count] for value in (*early, *late)]
    gram = jnp.concatenate(
        [
            jnp.concatenate([quarters[0], quarters[3]], axis=1),
            jnp.concatenate([quarters[2], quarters[1]], axis=1),
        ],
        axis=0,
    )
    first = jnp.concatenate([value[:outs] for value in early], axis=1)
    second = jnp.concatenate([value[:outs] for value in late], axis=1)
    second = second - STEP_RATE / total * jnp.dot(
        first, gram, precision=HIGHEST, preferred_element_type=jnp.float32
    )
    given, even = came[member[0]], member[0] < 2
    tiles[member[0]] = tile[0]
    tiles[member[0] ^ 1] = paired[...]
    tiles[member[0] ^ 2] = jnp.where(even, given, beside[...])
    tiles[member[0] ^ 3] = jnp.where(even, beside[...], given)
    update = None
    for t, residual in enumerate((first, second)):
        residuals[:, t, :] = residual
        rows = tiles[2 * t : 2 * t + 2].reshape(2 * count, -1)
        term = wide_dot(pieces_of(residual), rows, NN)
        update = term if update is None else update + term
    trained[...] = coefficients[...] - STEP_RATE / math.sqrt(total) * update


def call(kernel, out_shape, operands, scalars=0, out_kinds=None, in_place=(), scratch=()):
    outs = out_shape if isinstance(out_shape, tuple) else (out_shape,)
    out_kinds = out_kinds or [pltpu.VMEM] * len(outs)
    specs = tuple(pl.BlockSpec(memory_space=kind) for kind in out_kinds)
    kinds = [pltpu.SMEM] * scalars + [pltpu.VMEM] * (len(operands) - scalars)
    kinds = [pltpu.HBM if at in in_place else kind for at, kind in enumerate(kinds)]
    operands = [
        value if kind is pltpu.SMEM else pltpu.with_memory_space_constraint(value, kind)
        for value, kind in zip(operands, kinds)
    ]
    return pl.pallas_call(
        kernel,
        in_specs=[pl.BlockSpec(memory_space=kind) for kind in kinds],
        out_specs=specs if isinstance(out_shape, tuple) else specs[0],
        out_shape=out_shape,
        scratch_shapes=scratch,
        compiler_params=pltpu.CompilerParams(vmem_limit_bytes=SCRATCH),
    )(*operands)


def body(spectra, targets, centers, coefficients, owners, batch_rows):
    width, features = centers.shape
    outs = coefficients.shape[1]
    batch = batch_rows.shape[1]
    half = batch // 2
    total = width * lax.axis_size(AXES)
    sizes = tuple(lax.axis_size(name) for name in AXES)
    plane = sizes[0] * sizes[2]
    each = half // plane
    device = lax.axis_index(AXES).reshape(1)
    narrow = jnp.bfloat16
    z_size, core_size = sizes[1], sizes[3]
    member = ((lax.axis_index("z") & 1) * core_size + lax.axis_index("core")).reshape(1)

    def move(value, target):
        pairs = []
        for z in range(z_size):
            for c in range(core_size):
                to = target((z & 1) * core_size + c)
                pairs.append((z * core_size + c, (z - (z & 1) + to // 2) * core_size + to % 2))
        return lax.ppermute(value, ("z", "core"), pairs)

    def by(value, mask):
        return move(value, lambda at: at ^ mask)

    turned = coefficients.T
    shown = pltpu.VMEM((outs, batch), narrow)

    def rows_for(slots):
        blocks = pltpu.VMEM((plane, slots, each, features), narrow)
        extra = (shown, shown, pltpu.SMEM((1,), jnp.int32)) if slots == 1 else ()
        return call(
            functools.partial(rows_kernel, sizes=sizes),
            (blocks, blocks) + extra,
            (device, owners, batch_rows, spectra, targets.T),
            scalars=2,
            out_kinds=[pltpu.VMEM] * (2 + len(extra[:2])) + [pltpu.SMEM] * len(extra[2:]),
            in_place=(2, 3, 4),
            scratch=(
                pltpu.VMEM(spectra.shape, narrow),
                pltpu.VMEM(targets.shape[::-1], narrow),
                pltpu.VMEM(batch_rows.shape, jnp.int32),
                pltpu.SemaphoreType.DMA((CHUNKS + 2,)),
            ),
        )

    def scatter(kept, sent):
        return call(
            functools.partial(along_kernel, sizes=sizes),
            pltpu.VMEM((z_size, each, features), narrow),
            (owners, exchange(kept + by(sent, 1), PLANE)),
            scalars=1,
        )

    def reach(kept, sent):
        return exchange(scatter(kept, sent), "z")

    kept, sent, near, across, apart = rows_for(1)
    along = lax.cond(apart[0] != 0, lambda: reach(kept, sent), lambda: reach(*rows_for(2)))
    spread_out = call(
        functools.partial(spread_kernel, sizes=sizes),
        pltpu.VMEM((plane, each, features), narrow),
        (device, owners, along),
        scalars=2,
    )
    across, turned, spread_out = lax.optimization_barrier((across, turned, spread_out))
    gathered = exchange(spread_out, PLANE).reshape(half, features)
    near = near + by(across, 2)
    came_targets = by(near[:, half:], 1)

    both_centers = [centers, by(centers, 2)]
    both_coefficients = [turned, by(turned, 2)]
    pair_coefficients = by(both_coefficients[0], 1)
    all_centers = [both_centers[0], by(both_centers[0], 1), both_centers[1], by(both_centers[1], 1)]
    all_coefficients = [
        both_coefficients[0],
        pair_coefficients,
        both_coefficients[1],
        by(both_coefficients[1], 1),
    ]
    norms = [jnp.sqrt(squares(value) + EPSILON).reshape(1, -1) for value in all_centers]

    gathered, all_centers, all_coefficients, near, came_targets, norms = lax.optimization_barrier(
        (gathered, all_centers, all_coefficients, near, came_targets, norms)
    )
    square = pltpu.VMEM((GROUP, half, width), narrow)
    tile, turned_tile, side = call(
        functools.partial(tile_kernel, factor=math.sqrt(features)),
        (square, square, pltpu.VMEM((half, width), narrow)),
        (member, gathered, *all_centers, *norms),
        scalars=1,
    )
    came = move(tile, lambda at: at ^ 2 if at >= 2 else at ^ 3)
    partial = call(
        functools.partial(partial_kernel, root_scale=math.sqrt(total)),
        pltpu.VMEM((outs, half), jnp.float32),
        (turned_tile, *all_coefficients, near[:, :half], came_targets),
    )
    height = -(-(aligned(outs) + half) // (8 * plane)) * 8
    lines = call(
        join_kernel,
        pltpu.VMEM((plane * height, half), jnp.float32),
        (member, partial, tile, came),
        scalars=1,
    )
    paired = by(turned_tile[1], 1)
    beside = move(side, lambda at: at ^ 2 if at < 2 else at ^ 3)
    lines, paired, beside = lax.optimization_barrier((lines, paired, beside))
    own = exchange(lines.reshape(plane, height, half), PLANE).sum(axis=0)
    own = copies(own, "z").reshape(z_size // 2, 2, height, half).sum(axis=0)
    whole = copies(own, PLANE)
    trained, residuals = call(
        functools.partial(finish_kernel, total=total),
        (
            jax.ShapeDtypeStruct((outs, width), jnp.float32),
            jax.ShapeDtypeStruct((outs, ITERS, batch), jnp.float32),
        ),
        (member, whole, by(whole, 1), turned_tile, came, paired, beside, turned),
        scalars=1,
        scratch=(pltpu.VMEM((GROUP, half, width), narrow),),
    )
    return trained.T, jnp.transpose(residuals, (1, 2, 0))


def solution(mesh):
    torus = Mesh(mesh.devices.reshape(4, 8, 4, 2), AXES)
    return jax.shard_map(
        body,
        mesh=torus,
        in_specs=(P(AXES, None), P(AXES, None), P(AXES, None), P(AXES, None), P(), P()),
        out_specs=(P(AXES, None), P()),
        check_vma=False,
    )
```

```python
import functools
import math

import jax
import jax.numpy as jnp
from jax import lax
from jax.experimental import pallas as pl
from jax.experimental.pallas import tpu as pltpu
from jax.sharding import Mesh
from jax.sharding import PartitionSpec as P

ITERS = 2
AXES = ("y", "z", "x", "core")
PLANE = ("y", "x")
EPSILON = 1e-06
STEP_RATE = 0.2
PAIR = [(0, 1), (1, 0)]
Z_MASKS = (1, 2, 7)
SCRATCH = 16 << 20
CHUNKS = 4
HIGHEST = lax.Precision.HIGHEST
NT = (((1,), (1,)), ((), ()))
NN = (((1,), (0,)), ((), ()))


def swap(value):
    return lax.ppermute(value, "core", PAIR)


def exchange(blocks, axes):
    return lax.all_to_all(blocks, axes, 0, 0, tiled=True)


def place(device, sizes):
    bits = [size.bit_length() - 1 for size in sizes]
    core = device & (sizes[3] - 1)
    x = device >> bits[3] & (sizes[2] - 1)
    z = device >> (bits[3] + bits[2]) & (sizes[1] - 1)
    return device >> (bits[3] + bits[2] + bits[1]), z, x, core


def chosen(rows, held, own):
    spots = lax.broadcasted_iota(jnp.int32, (held, rows.shape[1]), 0) == rows
    return jnp.where(spots & own, 1.0, 0.0).astype(jnp.bfloat16)


def halves_of(batch_rows, t, core):
    rows = batch_rows[pl.ds(t, 1), :] if not isinstance(t, int) else batch_rows[t : t + 1, :]
    half = rows.shape[1] // 2
    first, second = rows[:, :half], rows[:, half:]
    return jnp.where(core == 0, first, second), jnp.where(core == 0, second, first)


def copies(value, axes):
    size = lax.axis_size(axes)
    return exchange(jnp.broadcast_to(value[None], (size, *value.shape)), axes)


def squares(value):
    return jnp.sum(jnp.square(value.astype(jnp.float32)), axis=1)


def aligned(size):
    return -(-size // 8) * 8


def rows_kernel(device, owners, batch_rows, spectra, kept, sent, *rest, sizes):
    flag, (lines, listed, arrivals) = rest[:-3], rest[-3:]
    here = device[0]
    core = here & (sizes[3] - 1)
    plane, slots, each, features = kept.shape
    chunk = features // CHUNKS
    later = owners[1] >> 1 == here >> 1
    involved = later | (owners[0] >> 1 == here >> 1)
    if flag:
        same_chip = owners[0] >> 1 == owners[1] >> 1
        same_z = place(owners[0], sizes)[1] == place(owners[1], sizes)[1]
        flag[0][0] = jnp.where(same_chip, 0, jnp.where(same_z, 1, 2))
        for t in range(ITERS):
            root_y, root_z, root_x, _ = place(owners[t], sizes)
            flag[1][t] = root_y * sizes[2] + root_x
            flag[1][ITERS + t] = root_z
        flag[1][2 * ITERS] = place(here, sizes)[1]

    @pl.when(involved)
    def _():
        listing = pltpu.make_async_copy(batch_rows, listed, arrivals.at[CHUNKS])
        listing.start()
        loads = []
        for at in range(CHUNKS):
            columns = slice(at * chunk, (at + 1) * chunk)
            load = pltpu.make_async_copy(
                spectra.at[:, columns], lines.at[:, columns], arrivals.at[at]
            )
            load.start()
            loads.append(load)
        listing.wait()
        spots = []
        for slot in range(slots):
            t = slot if slots > 1 else jnp.where(later, 1, 0)
            both = jnp.concatenate(halves_of(listed, t, core), axis=1)
            spots.append(chosen(both, lines.shape[0], owners[t] == here))
        spots = jnp.concatenate(spots, axis=1)
        for at in range(CHUNKS):
            columns = slice(at * chunk, (at + 1) * chunk)
            loads[at].wait()
            value = lax.dot_general(
                spots,
                lines[:, columns],
                (((0,), (0,)), ((), ())),
                preferred_element_type=jnp.float32,
            ).astype(kept.dtype)
            value = value.reshape(slots, 2, plane, each, chunk)
            for slot in range(slots):
                kept[:, slot, :, columns] = value[slot, 0]
                sent[:, slot, :, columns] = value[slot, 1]


def targets_kernel(device, owners, batch_rows, targets, kept, sent, *, sizes):
    here = device[0]
    core = here & (sizes[3] - 1)
    half = batch_rows.shape[1] // 2
    for t in range(ITERS):
        own = owners[t] == here
        for rows, out in zip(halves_of(batch_rows, t, core), (kept, sent)):
            out[:, t * half : (t + 1) * half] = jnp.dot(
                targets[...],
                chosen(rows, targets.shape[1], own),
                preferred_element_type=jnp.float32,
            ).astype(out.dtype)


def pick_kernel(spots, scattered, piece):
    slots = scattered.shape[1]
    for t in range(ITERS):
        block = scattered[spots[t], t if slots > 1 else 0]
        piece[t] = jnp.where(spots[ITERS + t] == spots[2 * ITERS], block, jnp.zeros_like(block))


def along_kernel(spots, scattered, out):
    at = jnp.where(spots[ITERS + 1] == spots[2 * ITERS], spots[1], spots[0])
    out[...] = jnp.broadcast_to(scattered[at, 0][None], out.shape)


def spread_kernel(spots, along, out, sent):
    copies_of = [
        pltpu.make_async_copy(along.at[spots[ITERS + t]], out.at[at, t], sent.at[at * ITERS + t])
        for at in range(out.shape[0])
        for t in range(ITERS)
    ]
    for copy in copies_of:
        copy.start()
    for copy in copies_of:
        copy.wait()


def spread_steps_kernel(piece, arrived, out):
    out[...] = jnp.broadcast_to((piece[...] + arrived[...])[None], out.shape)


def pieces_of(value):
    pieces = []
    for _ in range(3):
        piece = value.astype(jnp.bfloat16)
        pieces.append(piece)
        value = value - piece.astype(jnp.float32)
    return pieces


def wide_dot(pieces, value, dims):
    total = None
    for piece in reversed(pieces):
        term = lax.dot_general(piece, value, dims, preferred_element_type=jnp.float32)
        total = term if total is None else total + term
    return total


def tile_kernel(batch, own, other, own_norms, other_norms, tile, *, each, factor):
    lines = batch[...]
    norms = jnp.sqrt(
        jnp.sum(jnp.square(lines.astype(jnp.float32)), axis=1, keepdims=True) + EPSILON
    )
    count = lines.shape[0] // ITERS
    width = own.shape[0]
    for at, (centers, center_norms) in enumerate(((own, own_norms), (other, other_norms))):
        dots = lax.dot_general(lines, centers[...], NT, preferred_element_type=jnp.float32)
        scaled = dots / (norms * center_norms[...]) * factor
        value = scaled + scaled * scaled * scaled / 3.0
        value = value.reshape(count // each, ITERS, each, width)
        for t in range(ITERS):
            tile[t, :, at * width : (at + 1) * width] = (
                value[:, t].reshape(count, width).astype(tile.dtype)
            )


def partial_kernel(tile, own, other, kept, arrived, lines, *, root_scale):
    outs, width = own.shape
    count = tile.shape[1]
    step = aligned(outs)
    held = kept[...].astype(jnp.float32) + arrived[...].astype(jnp.float32)
    own_pieces, other_pieces = pieces_of(own[...]), pieces_of(other[...])
    for t in range(ITERS):
        total = wide_dot(own_pieces, tile[t, :, :width], NT) + wide_dot(
            other_pieces, tile[t, :, width:], NT
        )
        lines[t * step : t * step + outs, :] = (
            total / root_scale - held[:, t * count : (t + 1) * count]
        )
        lines[t * step + outs : (t + 1) * step, :] = jnp.zeros((step - outs, count), jnp.float32)


def join_kernel(core, partial, tile, came, lines):
    height, count = partial.shape
    width = tile.shape[2] // 2
    lines[:height, :] = partial[...]
    lines[height + 2 * count :, :] = jnp.zeros(
        (lines.shape[0] - height - 2 * count, count), jnp.float32
    )
    theirs = jnp.concatenate([came[0, :, width:], came[0, :, :width]], axis=1)
    gram = [
        lax.dot_general(value, tile[1], NT, preferred_element_type=jnp.float32)
        for value in (tile[0], theirs)
    ]
    is_first = core[0] == 0
    lines[height : height + count, :] = jnp.where(is_first, gram[0], gram[1])
    lines[height + count : height + 2 * count, :] = jnp.where(is_first, gram[1], gram[0])


def finish_kernel(core, mine, other, tile, came, coefficients, trained, residuals, *, total):
    outs, width = coefficients.shape
    count = mine.shape[1]
    step = aligned(outs)
    is_first = core[0] == 0

    def both(start, size):
        kept, sent = mine[start : start + size, :], other[start : start + size, :]
        return jnp.concatenate(
            [jnp.where(is_first, kept, sent), jnp.where(is_first, sent, kept)], axis=1
        )

    first = both(0, outs)
    gram = both(2 * step, 2 * count)
    second = both(step, outs) - STEP_RATE / total * jnp.dot(
        first, gram, precision=HIGHEST, preferred_element_type=jnp.float32
    )
    update = None
    for t, residual in enumerate((first, second)):
        residuals[:, t, :] = residual
        kept, sent = tile[t, :, :width], came[t, :, width:]
        rows = jnp.concatenate(
            [jnp.where(is_first, kept, sent), jnp.where(is_first, sent, kept)], axis=0
        )
        term = wide_dot(pieces_of(residual), rows, NN)
        update = term if update is None else update + term
    trained[...] = coefficients[...] - STEP_RATE / math.sqrt(total) * update


def call(kernel, out_shape, operands, scalars=0, out_kinds=None, in_place=(), in_smem=(), scratch=()):
    outs = out_shape if isinstance(out_shape, tuple) else (out_shape,)
    out_kinds = out_kinds or [pltpu.VMEM] * len(outs)
    specs = tuple(pl.BlockSpec(memory_space=kind) for kind in out_kinds)
    kinds = [pltpu.SMEM] * scalars + [pltpu.VMEM] * (len(operands) - scalars)
    kinds = [pltpu.HBM if at in in_place else kind for at, kind in enumerate(kinds)]
    operands = [
        value
        if kind is pltpu.SMEM and at not in in_smem
        else pltpu.with_memory_space_constraint(value, kind)
        for at, (value, kind) in enumerate(zip(operands, kinds))
    ]
    return pl.pallas_call(
        kernel,
        in_specs=[pl.BlockSpec(memory_space=kind) for kind in kinds],
        out_specs=specs if isinstance(out_shape, tuple) else specs[0],
        out_shape=out_shape,
        scratch_shapes=scratch,
        compiler_params=pltpu.CompilerParams(vmem_limit_bytes=SCRATCH),
    )(*operands)


def body(spectra, targets, centers, coefficients, owners, batch_rows):
    width, features = centers.shape
    outs = coefficients.shape[1]
    batch = batch_rows.shape[1]
    half = batch // 2
    total = width * lax.axis_size(AXES)
    sizes = tuple(lax.axis_size(name) for name in AXES)
    plane = sizes[0] * sizes[2]
    each = half // plane
    device = lax.axis_index(AXES).reshape(1)
    core = lax.axis_index("core").reshape(1)
    narrow = jnp.bfloat16
    block = pltpu.VMEM((ITERS, each, features), narrow)
    whole_block = jax.ShapeDtypeStruct((plane, ITERS, each, features), narrow)

    def rows_for(slots):
        blocks = pltpu.VMEM((plane, slots, each, features), narrow)
        flag = (pltpu.SMEM((1,), jnp.int32), pltpu.SMEM((8,), jnp.int32)) if slots == 1 else ()
        return call(
            functools.partial(rows_kernel, sizes=sizes),
            (blocks, blocks) + flag,
            (device, owners, batch_rows, spectra),
            scalars=2,
            out_kinds=[pltpu.VMEM, pltpu.VMEM] + [pltpu.SMEM] * len(flag),
            in_place=(2, 3),
            scratch=(
                pltpu.VMEM(spectra.shape, narrow),
                pltpu.VMEM(batch_rows.shape, jnp.int32),
                pltpu.SemaphoreType.DMA((CHUNKS + 1,)),
            ),
        )

    def in_steps(kept, sent):
        piece = call(
            pick_kernel,
            block,
            (spots, exchange(kept + swap(sent), PLANE)),
            scalars=1,
            in_smem=(0,),
        )
        arrived = None
        for mask in Z_MASKS:
            piece = piece if arrived is None else piece + arrived
            arrived = lax.ppermute(piece, "z", [(i, i ^ mask) for i in range(sizes[1])])
        return call(spread_steps_kernel, whole_block, (piece, arrived))

    def at_once(kept, sent):
        along = call(
            along_kernel,
            pltpu.VMEM((sizes[1], each, features), narrow),
            (spots, exchange(kept + swap(sent), PLANE)),
            scalars=1,
            in_smem=(0,),
        )
        return call(
            spread_kernel,
            whole_block,
            (spots, exchange(along, "z")),
            scalars=1,
            in_smem=(0,),
            out_kinds=[pltpu.HBM],
            scratch=(pltpu.SemaphoreType.DMA((plane * ITERS,)),),
        )

    kept, sent, apart, spots = rows_for(1)
    spread_out = lax.switch(
        apart[0],
        (lambda: in_steps(*rows_for(2)), lambda: in_steps(kept, sent), lambda: at_once(kept, sent)),
    )
    gathered = exchange(spread_out, PLANE).reshape(ITERS * half, features)

    shown = pltpu.VMEM((outs, ITERS * half), narrow)
    kept_targets, sent_targets = call(
        functools.partial(targets_kernel, sizes=sizes),
        (shown, shown),
        (device, owners, batch_rows, targets.T),
        scalars=2,
    )
    came_targets = swap(sent_targets)

    turned = coefficients.T
    turned_other = swap(turned)
    other_centers = swap(centers)
    norms = [jnp.sqrt(squares(value) + EPSILON).reshape(1, -1) for value in (centers, other_centers)]

    tile = call(
        functools.partial(tile_kernel, each=each, factor=math.sqrt(features)),
        pltpu.VMEM((ITERS, half, 2 * width), narrow),
        (gathered, centers, other_centers, *norms),
    )
    came = swap(tile)
    height = -(-(2 * aligned(outs) + batch) // (8 * plane)) * 8
    partial = call(
        functools.partial(partial_kernel, root_scale=math.sqrt(total)),
        pltpu.VMEM((2 * aligned(outs), half), jnp.float32),
        (tile, turned, turned_other, kept_targets, came_targets),
    )
    lines = call(
        join_kernel,
        pltpu.VMEM((plane * height, half), jnp.float32),
        (core, partial, tile, came),
        scalars=1,
    )
    own = exchange(lines.reshape(plane, height, half), PLANE).sum(axis=0)
    own = copies(own, "z").sum(axis=0)
    whole = copies(own, PLANE).reshape(plane * height, half)
    trained, residuals = call(
        functools.partial(finish_kernel, total=total),
        (
            jax.ShapeDtypeStruct((outs, width), jnp.float32),
            jax.ShapeDtypeStruct((outs, ITERS, batch), jnp.float32),
        ),
        (core, whole, swap(whole), tile, came, turned),
        scalars=1,
    )
    return trained.T, jnp.transpose(residuals, (1, 2, 0))


def solution(mesh):
    torus = Mesh(mesh.devices.reshape(4, 8, 4, 2), AXES)
    return jax.shard_map(
        body,
        mesh=torus,
        in_specs=(P(AXES, None), P(AXES, None), P(AXES, None), P(AXES, None), P(), P()),
        out_specs=(P(AXES, None), P()),
        check_vma=False,
    )
```

```python
import functools
import math

import jax
import jax.numpy as jnp
from jax import lax
from jax.experimental import pallas as pl
from jax.experimental.pallas import tpu as pltpu
from jax.sharding import Mesh
from jax.sharding import PartitionSpec as P

ITERS = 2
AXES = ("y", "z", "x", "core")
PLANE = ("y", "x")
EPSILON = 1e-06
STEP_RATE = 0.2
PAIR = [(0, 1), (1, 0)]
Z_MASKS = (1, 2, 7)
SCRATCH = 16 << 20
CHUNKS = 4
HIGHEST = lax.Precision.HIGHEST
NT = (((1,), (1,)), ((), ()))
NN = (((1,), (0,)), ((), ()))


def swap(value):
    return lax.ppermute(value, "core", PAIR)


def exchange(blocks, axes):
    return lax.all_to_all(blocks, axes, 0, 0, tiled=True)


def place(device, sizes):
    bits = [size.bit_length() - 1 for size in sizes]
    core = device & (sizes[3] - 1)
    x = device >> bits[3] & (sizes[2] - 1)
    z = device >> (bits[3] + bits[2]) & (sizes[1] - 1)
    return device >> (bits[3] + bits[2] + bits[1]), z, x, core


def chosen(rows, held, own):
    spots = lax.broadcasted_iota(jnp.int32, (held, rows.shape[1]), 0) == rows
    return jnp.where(spots & own, 1.0, 0.0).astype(jnp.bfloat16)


def halves_of(batch_rows, t, core):
    rows = batch_rows[pl.ds(t, 1), :] if not isinstance(t, int) else batch_rows[t : t + 1, :]
    half = rows.shape[1] // 2
    first, second = rows[:, :half], rows[:, half:]
    return jnp.where(core == 0, first, second), jnp.where(core == 0, second, first)


def copies(value, axes):
    size = lax.axis_size(axes)
    return exchange(jnp.broadcast_to(value[None], (size, *value.shape)), axes)


def squares(value):
    return jnp.sum(jnp.square(value.astype(jnp.float32)), axis=1)


def aligned(size):
    return -(-size // 8) * 8


def rows_kernel(device, owners, batch_rows, spectra, kept, sent, *rest, sizes):
    flag, (lines, listed, arrivals) = rest[:-3], rest[-3:]
    here = device[0]
    core = here & (sizes[3] - 1)
    plane, slots, each, features = kept.shape
    chunk = features // CHUNKS
    later = owners[1] >> 1 == here >> 1
    involved = later | (owners[0] >> 1 == here >> 1)
    if flag:
        same_chip = owners[0] >> 1 == owners[1] >> 1
        same_z = place(owners[0], sizes)[1] == place(owners[1], sizes)[1]
        flag[0][0] = jnp.where(same_chip, 0, jnp.where(same_z, 1, 2))
        for t in range(ITERS):
            root_y, root_z, root_x, _ = place(owners[t], sizes)
            flag[1][t] = root_y * sizes[2] + root_x
            flag[1][ITERS + t] = root_z
        flag[1][2 * ITERS] = place(here, sizes)[1]

    @pl.when(involved)
    def _():
        listing = pltpu.make_async_copy(batch_rows, listed, arrivals.at[CHUNKS])
        listing.start()
        loads = []
        for at in range(CHUNKS):
            columns = slice(at * chunk, (at + 1) * chunk)
            load = pltpu.make_async_copy(
                spectra.at[:, columns], lines.at[:, columns], arrivals.at[at]
            )
            load.start()
            loads.append(load)
        listing.wait()
        spots = []
        for slot in range(slots):
            t = slot if slots > 1 else jnp.where(later, 1, 0)
            both = jnp.concatenate(halves_of(listed, t, core), axis=1)
            spots.append(chosen(both, lines.shape[0], owners[t] == here))
        spots = jnp.concatenate(spots, axis=1)
        for at in range(CHUNKS):
            columns = slice(at * chunk, (at + 1) * chunk)
            loads[at].wait()
            value = lax.dot_general(
                spots,
                lines[:, columns],
                (((0,), (0,)), ((), ())),
                preferred_element_type=jnp.float32,
            ).astype(kept.dtype)
            value = value.reshape(slots, 2, plane, each, chunk)
            for slot in range(slots):
                kept[:, slot, :, columns] = value[slot, 0]
                sent[:, slot, :, columns] = value[slot, 1]


def targets_kernel(device, owners, batch_rows, targets, kept, sent, *, sizes):
    here = device[0]
    core = here & (sizes[3] - 1)
    half = batch_rows.shape[1] // 2
    for t in range(ITERS):
        own = owners[t] == here
        for rows, out in zip(halves_of(batch_rows, t, core), (kept, sent)):
            out[:, t * half : (t + 1) * half] = jnp.dot(
                targets[...],
                chosen(rows, targets.shape[1], own),
                preferred_element_type=jnp.float32,
            ).astype(out.dtype)


def pick_kernel(spots, scattered, piece):
    slots = scattered.shape[1]
    for t in range(ITERS):
        block = scattered[spots[t], t if slots > 1 else 0]
        piece[t] = jnp.where(spots[ITERS + t] == spots[2 * ITERS], block, jnp.zeros_like(block))


def along_kernel(spots, scattered, out):
    at = jnp.where(spots[ITERS + 1] == spots[2 * ITERS], spots[1], spots[0])
    out[...] = jnp.broadcast_to(scattered[at, 0][None], out.shape)


def spread_kernel(spots, along, out, sent):
    copies_of = [
        pltpu.make_async_copy(along.at[spots[ITERS + t]], out.at[at, t], sent.at[at * ITERS + t])
        for at in range(out.shape[0])
        for t in range(ITERS)
    ]
    for copy in copies_of:
        copy.start()
    for copy in copies_of:
        copy.wait()


def spread_steps_kernel(piece, arrived, out):
    out[...] = jnp.broadcast_to((piece[...] + arrived[...])[None], out.shape)


def pieces_of(value):
    pieces = []
    for _ in range(3):
        piece = value.astype(jnp.bfloat16)
        pieces.append(piece)
        value = value - piece.astype(jnp.float32)
    return pieces


def wide_dot(pieces, value, dims):
    total = None
    for piece in reversed(pieces):
        term = lax.dot_general(piece, value, dims, preferred_element_type=jnp.float32)
        total = term if total is None else total + term
    return total


def tile_kernel(batch, own, other, own_norms, other_norms, tile, *, each, factor):
    lines = batch[...]
    norms = jnp.sqrt(
        jnp.sum(jnp.square(lines.astype(jnp.float32)), axis=1, keepdims=True) + EPSILON
    )
    count = lines.shape[0] // ITERS
    width = own.shape[0]
    for at, (centers, center_norms) in enumerate(((own, own_norms), (other, other_norms))):
        dots = lax.dot_general(lines, centers[...], NT, preferred_element_type=jnp.float32)
        scaled = dots / (norms * center_norms[...]) * factor
        value = scaled + scaled * scaled * scaled / 3.0
        value = value.reshape(count // each, ITERS, each, width)
        for t in range(ITERS):
            tile[t, :, at * width : (at + 1) * width] = (
                value[:, t].reshape(count, width).astype(tile.dtype)
            )


def partial_kernel(tile, own, other, kept, arrived, lines, *, root_scale):
    outs, width = own.shape
    count = tile.shape[1]
    step = aligned(outs)
    held = kept[...].astype(jnp.float32) + arrived[...].astype(jnp.float32)
    own_pieces, other_pieces = pieces_of(own[...]), pieces_of(other[...])
    for t in range(ITERS):
        total = wide_dot(own_pieces, tile[t, :, :width], NT) + wide_dot(
            other_pieces, tile[t, :, width:], NT
        )
        lines[t * step : t * step + outs, :] = (
            total / root_scale - held[:, t * count : (t + 1) * count]
        )
        lines[t * step + outs : (t + 1) * step, :] = jnp.zeros((step - outs, count), jnp.float32)


def join_kernel(core, partial, tile, came, lines):
    height, count = partial.shape
    width = tile.shape[2] // 2
    lines[:height, :] = partial[...]
    lines[height + 2 * count :, :] = jnp.zeros(
        (lines.shape[0] - height - 2 * count, count), jnp.float32
    )
    theirs = jnp.concatenate([came[0, :, width:], came[0, :, :width]], axis=1)
    gram = [
        lax.dot_general(value, tile[1], NT, preferred_element_type=jnp.float32)
        for value in (tile[0], theirs)
    ]
    is_first = core[0] == 0
    lines[height : height + count, :] = jnp.where(is_first, gram[0], gram[1])
    lines[height + count : height + 2 * count, :] = jnp.where(is_first, gram[1], gram[0])


def finish_kernel(core, mine, other, tile, came, coefficients, trained, residuals, shown, sent, *, total):
    outs, width = coefficients.shape
    count = mine.shape[1]
    step = aligned(outs)
    is_first = core[0] == 0

    def both(start, size):
        kept, sent = mine[start : start + size, :], other[start : start + size, :]
        return jnp.concatenate(
            [jnp.where(is_first, kept, sent), jnp.where(is_first, sent, kept)], axis=1
        )

    first = both(0, outs)
    gram = both(2 * step, 2 * count)
    second = both(step, outs) - STEP_RATE / total * jnp.dot(
        first, gram, precision=HIGHEST, preferred_element_type=jnp.float32
    )
    for t, residual in enumerate((first, second)):
        shown[:, t, :] = residual
    leaving = pltpu.make_async_copy(shown, residuals, sent)
    leaving.start()
    update = None
    for t, residual in enumerate((first, second)):
        kept, sent = tile[t, :, :width], came[t, :, width:]
        rows = jnp.concatenate(
            [jnp.where(is_first, kept, sent), jnp.where(is_first, sent, kept)], axis=0
        )
        term = wide_dot(pieces_of(residual), rows, NN)
        update = term if update is None else update + term
    trained[...] = coefficients[...] - STEP_RATE / math.sqrt(total) * update
    leaving.wait()


def call(kernel, out_shape, operands, scalars=0, out_kinds=None, in_place=(), in_smem=(), scratch=()):
    outs = out_shape if isinstance(out_shape, tuple) else (out_shape,)
    out_kinds = out_kinds or [pltpu.VMEM] * len(outs)
    specs = tuple(pl.BlockSpec(memory_space=kind) for kind in out_kinds)
    kinds = [pltpu.SMEM] * scalars + [pltpu.VMEM] * (len(operands) - scalars)
    kinds = [pltpu.HBM if at in in_place else kind for at, kind in enumerate(kinds)]
    operands = [
        value
        if kind is pltpu.SMEM and at not in in_smem
        else pltpu.with_memory_space_constraint(value, kind)
        for at, (value, kind) in enumerate(zip(operands, kinds))
    ]
    return pl.pallas_call(
        kernel,
        in_specs=[pl.BlockSpec(memory_space=kind) for kind in kinds],
        out_specs=specs if isinstance(out_shape, tuple) else specs[0],
        out_shape=out_shape,
        scratch_shapes=scratch,
        compiler_params=pltpu.CompilerParams(vmem_limit_bytes=SCRATCH),
    )(*operands)


def body(spectra, targets, centers, coefficients, owners, batch_rows):
    width, features = centers.shape
    outs = coefficients.shape[1]
    batch = batch_rows.shape[1]
    half = batch // 2
    total = width * lax.axis_size(AXES)
    sizes = tuple(lax.axis_size(name) for name in AXES)
    plane = sizes[0] * sizes[2]
    each = half // plane
    device = lax.axis_index(AXES).reshape(1)
    core = lax.axis_index("core").reshape(1)
    narrow = jnp.bfloat16
    block = pltpu.VMEM((ITERS, each, features), narrow)
    whole_block = jax.ShapeDtypeStruct((plane, ITERS, each, features), narrow)

    def rows_for(slots):
        blocks = pltpu.VMEM((plane, slots, each, features), narrow)
        flag = (pltpu.SMEM((1,), jnp.int32), pltpu.SMEM((8,), jnp.int32)) if slots == 1 else ()
        return call(
            functools.partial(rows_kernel, sizes=sizes),
            (blocks, blocks) + flag,
            (device, owners, batch_rows, spectra),
            scalars=2,
            out_kinds=[pltpu.VMEM, pltpu.VMEM] + [pltpu.SMEM] * len(flag),
            in_place=(2, 3),
            scratch=(
                pltpu.VMEM(spectra.shape, narrow),
                pltpu.VMEM(batch_rows.shape, jnp.int32),
                pltpu.SemaphoreType.DMA((CHUNKS + 1,)),
            ),
        )

    def in_steps(kept, sent):
        piece = call(
            pick_kernel,
            block,
            (spots, exchange(kept + swap(sent), PLANE)),
            scalars=1,
            in_smem=(0,),
        )
        arrived = None
        for mask in Z_MASKS:
            piece = piece if arrived is None else piece + arrived
            arrived = lax.ppermute(piece, "z", [(i, i ^ mask) for i in range(sizes[1])])
        return call(spread_steps_kernel, whole_block, (piece, arrived))

    def at_once(kept, sent):
        along = call(
            along_kernel,
            pltpu.VMEM((sizes[1], each, features), narrow),
            (spots, exchange(kept + swap(sent), PLANE)),
            scalars=1,
            in_smem=(0,),
        )
        return call(
            spread_kernel,
            whole_block,
            (spots, exchange(along, "z")),
            scalars=1,
            in_smem=(0,),
            out_kinds=[pltpu.HBM],
            scratch=(pltpu.SemaphoreType.DMA((plane * ITERS,)),),
        )

    kept, sent, apart, spots = rows_for(1)
    spread_out = lax.switch(
        apart[0],
        (lambda: in_steps(*rows_for(2)), lambda: in_steps(kept, sent), lambda: at_once(kept, sent)),
    )
    gathered = exchange(spread_out, PLANE).reshape(ITERS * half, features)

    shown = pltpu.VMEM((outs, ITERS * half), narrow)
    kept_targets, sent_targets = call(
        functools.partial(targets_kernel, sizes=sizes),
        (shown, shown),
        (device, owners, batch_rows, targets.T),
        scalars=2,
    )
    came_targets = swap(sent_targets)

    turned = coefficients.T
    turned_other = swap(turned)
    other_centers = swap(centers)
    norms = [jnp.sqrt(squares(value) + EPSILON).reshape(1, -1) for value in (centers, other_centers)]

    tile = call(
        functools.partial(tile_kernel, each=each, factor=math.sqrt(features)),
        pltpu.VMEM((ITERS, half, 2 * width), narrow),
        (gathered, centers, other_centers, *norms),
    )
    came = swap(tile)
    height = -(-(2 * aligned(outs) + batch) // (8 * plane)) * 8
    partial = call(
        functools.partial(partial_kernel, root_scale=math.sqrt(total)),
        pltpu.VMEM((2 * aligned(outs), half), jnp.float32),
        (tile, turned, turned_other, kept_targets, came_targets),
    )
    lines = call(
        join_kernel,
        pltpu.VMEM((plane * height, half), jnp.float32),
        (core, partial, tile, came),
        scalars=1,
    )
    own = exchange(lines.reshape(plane, height, half), PLANE).sum(axis=0)
    own = copies(own, "z").sum(axis=0)
    whole = copies(own, PLANE).reshape(plane * height, half)
    trained, residuals = call(
        functools.partial(finish_kernel, total=total),
        (
            jax.ShapeDtypeStruct((outs, width), jnp.float32),
            jax.ShapeDtypeStruct((outs, ITERS, batch), jnp.float32),
        ),
        (core, whole, swap(whole), tile, came, turned),
        scalars=1,
        out_kinds=[pltpu.VMEM, pltpu.HBM],
        scratch=(
            pltpu.VMEM((outs, ITERS, batch), jnp.float32),
            pltpu.SemaphoreType.DMA(()),
        ),
    )
    return trained.T, jnp.transpose(residuals, (1, 2, 0))


def solution(mesh):
    torus = Mesh(mesh.devices.reshape(4, 8, 4, 2), AXES)
    return jax.shard_map(
        body,
        mesh=torus,
        in_specs=(P(AXES, None), P(AXES, None), P(AXES, None), P(AXES, None), P(), P()),
        out_specs=(P(AXES, None), P()),
        check_vma=False,
    )
```

```python
import functools
import math

import jax
import jax.numpy as jnp
from jax import lax
from jax.experimental import pallas as pl
from jax.experimental.pallas import tpu as pltpu
from jax.sharding import Mesh
from jax.sharding import PartitionSpec as P

ITERS = 2
AXES = ("y", "z", "x", "core")
PLANE = ("y", "x")
EPSILON = 1e-06
STEP_RATE = 0.2
PAIR = [(0, 1), (1, 0)]
Z_MASKS = (1, 2, 7)
SCRATCH = 16 << 20
CHUNKS = 4
HIGHEST = lax.Precision.HIGHEST
NT = (((1,), (1,)), ((), ()))
NN = (((1,), (0,)), ((), ()))


def swap(value):
    return lax.ppermute(value, "core", PAIR)


def exchange(blocks, axes):
    return lax.all_to_all(blocks, axes, 0, 0, tiled=True)


def place(device, sizes):
    bits = [size.bit_length() - 1 for size in sizes]
    core = device & (sizes[3] - 1)
    x = device >> bits[3] & (sizes[2] - 1)
    z = device >> (bits[3] + bits[2]) & (sizes[1] - 1)
    return device >> (bits[3] + bits[2] + bits[1]), z, x, core


def chosen(rows, held, own):
    spots = lax.broadcasted_iota(jnp.int32, (held, rows.shape[1]), 0) == rows
    return jnp.where(spots & own, 1.0, 0.0).astype(jnp.bfloat16)


def halves_of(batch_rows, t, core):
    rows = batch_rows[pl.ds(t, 1), :] if not isinstance(t, int) else batch_rows[t : t + 1, :]
    half = rows.shape[1] // 2
    first, second = rows[:, :half], rows[:, half:]
    return jnp.where(core == 0, first, second), jnp.where(core == 0, second, first)


def copies(value, axes):
    size = lax.axis_size(axes)
    return exchange(jnp.broadcast_to(value[None], (size, *value.shape)), axes)


def squares(value):
    return jnp.sum(jnp.square(value.astype(jnp.float32)), axis=1)


def aligned(size):
    return -(-size // 8) * 8


def rows_kernel(owners, batch_rows, spectra, kept, sent, *rest, sizes):
    flag, (lines, listed, arrivals) = rest[:-3], rest[-3:]
    here = lax.axis_index(AXES)
    core = here & (sizes[3] - 1)
    plane, slots, each, features = kept.shape
    chunk = features // CHUNKS
    later = owners[1] >> 1 == here >> 1
    involved = later | (owners[0] >> 1 == here >> 1)
    if flag:
        same_chip = owners[0] >> 1 == owners[1] >> 1
        same_z = place(owners[0], sizes)[1] == place(owners[1], sizes)[1]
        flag[0][0] = jnp.where(same_chip, 0, jnp.where(same_z, 1, 2))
        for t in range(ITERS):
            root_y, root_z, root_x, _ = place(owners[t], sizes)
            flag[1][t] = root_y * sizes[2] + root_x
            flag[1][ITERS + t] = root_z
        flag[1][2 * ITERS] = place(here, sizes)[1]

    @pl.when(involved)
    def _():
        listing = pltpu.make_async_copy(batch_rows, listed, arrivals.at[CHUNKS])
        listing.start()
        loads = []
        for at in range(CHUNKS):
            columns = slice(at * chunk, (at + 1) * chunk)
            load = pltpu.make_async_copy(
                spectra.at[:, columns], lines.at[:, columns], arrivals.at[at]
            )
            load.start()
            loads.append(load)
        listing.wait()
        spots = []
        for slot in range(slots):
            t = slot if slots > 1 else jnp.where(later, 1, 0)
            both = jnp.concatenate(halves_of(listed, t, core), axis=1)
            spots.append(chosen(both, lines.shape[0], owners[t] == here))
        spots = jnp.concatenate(spots, axis=1)
        for at in range(CHUNKS):
            columns = slice(at * chunk, (at + 1) * chunk)
            loads[at].wait()
            value = lax.dot_general(
                spots,
                lines[:, columns],
                (((0,), (0,)), ((), ())),
                preferred_element_type=jnp.float32,
            ).astype(kept.dtype)
            value = value.reshape(slots, 2, plane, each, chunk)
            for slot in range(slots):
                kept[:, slot, :, columns] = value[slot, 0]
                sent[:, slot, :, columns] = value[slot, 1]


def targets_kernel(device, owners, batch_rows, targets, kept, sent, *, sizes):
    here = device[0]
    core = here & (sizes[3] - 1)
    half = batch_rows.shape[1] // 2
    for t in range(ITERS):
        own = owners[t] == here
        for rows, out in zip(halves_of(batch_rows, t, core), (kept, sent)):
            out[:, t * half : (t + 1) * half] = jnp.dot(
                targets[...],
                chosen(rows, targets.shape[1], own),
                preferred_element_type=jnp.float32,
            ).astype(out.dtype)


def pick_kernel(spots, scattered, piece):
    slots = scattered.shape[1]
    for t in range(ITERS):
        block = scattered[spots[t], t if slots > 1 else 0]
        piece[t] = jnp.where(spots[ITERS + t] == spots[2 * ITERS], block, jnp.zeros_like(block))


def along_kernel(spots, scattered, out):
    at = jnp.where(spots[ITERS + 1] == spots[2 * ITERS], spots[1], spots[0])
    out[...] = jnp.broadcast_to(scattered[at, 0][None], out.shape)


def spread_kernel(spots, along, out, sent):
    copies_of = [
        pltpu.make_async_copy(along.at[spots[ITERS + t]], out.at[at, t], sent.at[at * ITERS + t])
        for at in range(out.shape[0])
        for t in range(ITERS)
    ]
    for copy in copies_of:
        copy.start()
    for copy in copies_of:
        copy.wait()


def spread_steps_kernel(piece, arrived, out):
    out[...] = jnp.broadcast_to((piece[...] + arrived[...])[None], out.shape)


def pieces_of(value):
    pieces = []
    for _ in range(3):
        piece = value.astype(jnp.bfloat16)
        pieces.append(piece)
        value = value - piece.astype(jnp.float32)
    return pieces


def wide_dot(pieces, value, dims):
    total = None
    for piece in reversed(pieces):
        term = lax.dot_general(piece, value, dims, preferred_element_type=jnp.float32)
        total = term if total is None else total + term
    return total


def tile_kernel(batch, own, other, own_norms, other_norms, tile, *, each, factor):
    lines = batch[...]
    norms = jnp.sqrt(
        jnp.sum(jnp.square(lines.astype(jnp.float32)), axis=1, keepdims=True) + EPSILON
    )
    count = lines.shape[0] // ITERS
    width = own.shape[0]
    for at, (centers, center_norms) in enumerate(((own, own_norms), (other, other_norms))):
        dots = lax.dot_general(lines, centers[...], NT, preferred_element_type=jnp.float32)
        scaled = dots / (norms * center_norms[...]) * factor
        value = scaled + scaled * scaled * scaled / 3.0
        value = value.reshape(count // each, ITERS, each, width)
        for t in range(ITERS):
            tile[t, :, at * width : (at + 1) * width] = (
                value[:, t].reshape(count, width).astype(tile.dtype)
            )


def partial_kernel(tile, own, other, kept, arrived, lines, *, root_scale):
    outs, width = own.shape
    count = tile.shape[1]
    step = aligned(outs)
    held = kept[...].astype(jnp.float32) + arrived[...].astype(jnp.float32)
    own_pieces, other_pieces = pieces_of(own[...]), pieces_of(other[...])
    for t in range(ITERS):
        total = wide_dot(own_pieces, tile[t, :, :width], NT) + wide_dot(
            other_pieces, tile[t, :, width:], NT
        )
        lines[t * step : t * step + outs, :] = (
            total / root_scale - held[:, t * count : (t + 1) * count]
        )
        lines[t * step + outs : (t + 1) * step, :] = jnp.zeros((step - outs, count), jnp.float32)


def join_kernel(core, partial, tile, came, lines):
    height, count = partial.shape
    width = tile.shape[2] // 2
    lines[:height, :] = partial[...]
    lines[height + 2 * count :, :] = jnp.zeros(
        (lines.shape[0] - height - 2 * count, count), jnp.float32
    )
    theirs = jnp.concatenate([came[0, :, width:], came[0, :, :width]], axis=1)
    gram = [
        lax.dot_general(value, tile[1], NT, preferred_element_type=jnp.float32)
        for value in (tile[0], theirs)
    ]
    is_first = core[0] == 0
    lines[height : height + count, :] = jnp.where(is_first, gram[0], gram[1])
    lines[height + count : height + 2 * count, :] = jnp.where(is_first, gram[1], gram[0])


def finish_kernel(core, mine, other, tile, came, coefficients, trained, residuals, *, total):
    outs, width = coefficients.shape
    count = mine.shape[1]
    step = aligned(outs)
    is_first = core[0] == 0

    def both(start, size):
        kept, sent = mine[start : start + size, :], other[start : start + size, :]
        return jnp.concatenate(
            [jnp.where(is_first, kept, sent), jnp.where(is_first, sent, kept)], axis=1
        )

    first = both(0, outs)
    gram = both(2 * step, 2 * count)
    second = both(step, outs) - STEP_RATE / total * jnp.dot(
        first, gram, precision=HIGHEST, preferred_element_type=jnp.float32
    )
    update = None
    for t, residual in enumerate((first, second)):
        residuals[:, t, :] = residual
        kept, sent = tile[t, :, :width], came[t, :, width:]
        rows = jnp.concatenate(
            [jnp.where(is_first, kept, sent), jnp.where(is_first, sent, kept)], axis=0
        )
        term = wide_dot(pieces_of(residual), rows, NN)
        update = term if update is None else update + term
    trained[...] = coefficients[...] - STEP_RATE / math.sqrt(total) * update


def call(kernel, out_shape, operands, scalars=0, out_kinds=None, in_place=(), in_smem=(), scratch=()):
    outs = out_shape if isinstance(out_shape, tuple) else (out_shape,)
    out_kinds = out_kinds or [pltpu.VMEM] * len(outs)
    specs = tuple(pl.BlockSpec(memory_space=kind) for kind in out_kinds)
    kinds = [pltpu.SMEM] * scalars + [pltpu.VMEM] * (len(operands) - scalars)
    kinds = [pltpu.HBM if at in in_place else kind for at, kind in enumerate(kinds)]
    operands = [
        value
        if kind is pltpu.SMEM and at not in in_smem
        else pltpu.with_memory_space_constraint(value, kind)
        for at, (value, kind) in enumerate(zip(operands, kinds))
    ]
    return pl.pallas_call(
        kernel,
        in_specs=[pl.BlockSpec(memory_space=kind) for kind in kinds],
        out_specs=specs if isinstance(out_shape, tuple) else specs[0],
        out_shape=out_shape,
        scratch_shapes=scratch,
        compiler_params=pltpu.CompilerParams(vmem_limit_bytes=SCRATCH),
    )(*operands)


def body(spectra, targets, centers, coefficients, owners, batch_rows):
    width, features = centers.shape
    outs = coefficients.shape[1]
    batch = batch_rows.shape[1]
    half = batch // 2
    total = width * lax.axis_size(AXES)
    sizes = tuple(lax.axis_size(name) for name in AXES)
    plane = sizes[0] * sizes[2]
    each = half // plane
    device = lax.axis_index(AXES).reshape(1)
    core = lax.axis_index("core").reshape(1)
    narrow = jnp.bfloat16
    block = pltpu.VMEM((ITERS, each, features), narrow)
    whole_block = jax.ShapeDtypeStruct((plane, ITERS, each, features), narrow)

    def rows_for(slots):
        blocks = pltpu.VMEM((plane, slots, each, features), narrow)
        flag = (pltpu.SMEM((1,), jnp.int32), pltpu.SMEM((8,), jnp.int32)) if slots == 1 else ()
        return call(
            functools.partial(rows_kernel, sizes=sizes),
            (blocks, blocks) + flag,
            (owners, batch_rows, spectra),
            scalars=1,
            out_kinds=[pltpu.VMEM, pltpu.VMEM] + [pltpu.SMEM] * len(flag),
            in_place=(1, 2),
            scratch=(
                pltpu.VMEM(spectra.shape, narrow),
                pltpu.VMEM(batch_rows.shape, jnp.int32),
                pltpu.SemaphoreType.DMA((CHUNKS + 1,)),
            ),
        )

    def in_steps(kept, sent):
        piece = call(
            pick_kernel,
            block,
            (spots, exchange(kept + swap(sent), PLANE)),
            scalars=1,
            in_smem=(0,),
        )
        arrived = None
        for mask in Z_MASKS:
            piece = piece if arrived is None else piece + arrived
            arrived = lax.ppermute(piece, "z", [(i, i ^ mask) for i in range(sizes[1])])
        return call(spread_steps_kernel, whole_block, (piece, arrived))

    def at_once(kept, sent):
        along = call(
            along_kernel,
            pltpu.VMEM((sizes[1], each, features), narrow),
            (spots, exchange(kept + swap(sent), PLANE)),
            scalars=1,
            in_smem=(0,),
        )
        return call(
            spread_kernel,
            whole_block,
            (spots, exchange(along, "z")),
            scalars=1,
            in_smem=(0,),
            out_kinds=[pltpu.HBM],
            scratch=(pltpu.SemaphoreType.DMA((plane * ITERS,)),),
        )

    kept, sent, apart, spots = rows_for(1)
    spread_out = lax.switch(
        apart[0],
        (lambda: in_steps(*rows_for(2)), lambda: in_steps(kept, sent), lambda: at_once(kept, sent)),
    )
    gathered = exchange(spread_out, PLANE).reshape(ITERS * half, features)

    shown = pltpu.VMEM((outs, ITERS * half), narrow)
    kept_targets, sent_targets = call(
        functools.partial(targets_kernel, sizes=sizes),
        (shown, shown),
        (device, owners, batch_rows, targets.T),
        scalars=2,
    )
    came_targets = swap(sent_targets)

    turned = coefficients.T
    turned_other = swap(turned)
    other_centers = swap(centers)
    norms = [jnp.sqrt(squares(value) + EPSILON).reshape(1, -1) for value in (centers, other_centers)]

    tile = call(
        functools.partial(tile_kernel, each=each, factor=math.sqrt(features)),
        pltpu.VMEM((ITERS, half, 2 * width), narrow),
        (gathered, centers, other_centers, *norms),
    )
    came = swap(tile)
    height = -(-(2 * aligned(outs) + batch) // (8 * plane)) * 8
    partial = call(
        functools.partial(partial_kernel, root_scale=math.sqrt(total)),
        pltpu.VMEM((2 * aligned(outs), half), jnp.float32),
        (tile, turned, turned_other, kept_targets, came_targets),
    )
    lines = call(
        join_kernel,
        pltpu.VMEM((plane * height, half), jnp.float32),
        (core, partial, tile, came),
        scalars=1,
    )
    own = exchange(lines.reshape(plane, height, half), PLANE).sum(axis=0)
    own = copies(own, "z").sum(axis=0)
    whole = copies(own, PLANE).reshape(plane * height, half)
    trained, residuals = call(
        functools.partial(finish_kernel, total=total),
        (
            jax.ShapeDtypeStruct((outs, width), jnp.float32),
            jax.ShapeDtypeStruct((outs, ITERS, batch), jnp.float32),
        ),
        (core, whole, swap(whole), tile, came, turned),
        scalars=1,
    )
    return trained.T, jnp.transpose(residuals, (1, 2, 0))


def solution(mesh):
    torus = Mesh(mesh.devices.reshape(4, 8, 4, 2), AXES)
    return jax.shard_map(
        body,
        mesh=torus,
        in_specs=(P(AXES, None), P(AXES, None), P(AXES, None), P(AXES, None), P(), P()),
        out_specs=(P(AXES, None), P()),
        check_vma=False,
    )
```
